256 devices in a mesh: isl: 16 (over z_lo, x), par: 2 (over z_hi), sp: 8 (over y, core).
Axes of the slice: x: 4, y: 4, z: 8 (z_hi: 2, z_lo: 4; z = z_hi * 4 + z_lo), core: 2. Of those that a mesh axis runs over, the one named last changes fastest.
Arguments:
- ensemble: float32 [16, 2, 4, 32, 32, 512], P('isl', 'par', None, 'sp'), may hold values from -6 to 6
- observations: float32 [32, 512], P('sp'), may hold values from -6 to 6
- obs_precision: float32 [32, 512], P('sp'), may hold values from 0.002 to 0.02
- island_ancestor: int32 [16], replicated, may hold values from 0 to 15, as said below
- particle_ancestor: int32 [16, 2], P('isl', 'par'), may hold values from 0 to 1, as said below
Outputs:
- resampled: float32 [16, 2, 4, 32, 32, 512], P('isl', 'par', None, 'sp')
- particle_logw: float32 [16, 2], P('isl', 'par')
- island_logw: float32 [16], P('isl')
The draws below stay inside these ranges and needn't reach their ends.
Inputs may be any that keep to these rules, and one draw needn't show every extreme that they name: island_ancestor names island 16 - 1 and island 0 in every draw. Every row of particle_ancestor names particle 0 and particle 2 - 1.
All inputs are finite; a program needn't handle non-finite values.
Results may differ from the reference program's by a relative error of at most 0.000069.
Values sent between devices are 32-bit elements; how exact they have to be, the bound alone decides.
A program may use at most 64 MiB of HBM per device.

```python
import math
import jax
import jax.numpy as jnp
from jax import lax

NZ = 32
NY = 512
FIELDS = 4
SWEEPS = 8
ISLANDS = 16
PER_ISL = 2
NX = 32


def draw_island_ancestor(key, part):
    first_key, second_key = jax.random.split(jax.random.fold_in(key, 17))
    parents = jax.random.randint(first_key, (ISLANDS,), 0, ISLANDS)
    ranking = jax.random.permutation(second_key, ISLANDS)
    parents = parents.at[ranking[0]].set(ISLANDS - 1)
    parents = parents.at[ranking[1]].set(0)
    return parents.astype(jnp.int32)


def draw_particle_ancestor(key, part):
    first_key, second_key = jax.random.split(jax.random.fold_in(key, 29))
    parents = jax.random.randint(first_key, (ISLANDS, PER_ISL), 0, PER_ISL)
    columns = jnp.arange(PER_ISL, dtype=jnp.int32)[None, :]
    scores = jax.random.randint(second_key, (ISLANDS, PER_ISL), 0, 1 << 20) * PER_ISL + columns
    ranking = jnp.argsort(scores, axis=1, stable=True)
    parents = jnp.where(columns == ranking[:, 0:1], PER_ISL - 1, parents)
    parents = jnp.where(columns == ranking[:, 1:2], 0, parents)
    return parents.astype(jnp.int32)


def steps_of(own_key, dims, shards, least, high):
    def one(dim, shards_of):
        steps = jax.random.uniform(jax.random.fold_in(jax.random.fold_in(own_key, 6), dim), (shards_of,), jnp.float32, least / len(shards), high / len(shards))
        return jnp.repeat(jnp.exp(steps), dims[dim] // shards_of).reshape((-1,) + (1,) * (len(dims) - dim - 1))

    loudness = one(*shards[0])
    for cut in shards[1:]:
        loudness = loudness * one(*cut)
    return loudness


def centred(rng, dims, spread, reach, shards=(), kind=jnp.bfloat16):
    values = jax.random.normal(rng, dims, jnp.float32) * spread
    if len(shards) > 0:
        values = steps_of(rng, dims, shards, -0.22, 0.18) * values
    return jnp.clip(values, min=-reach, max=reach).astype(kind)


def setup_inputs(seed: int = 0) -> dict:
    key_list = jax.random.split(jax.random.key(seed), 6)
    ensemble = centred(key_list[0], (ISLANDS, PER_ISL, FIELDS, NX, NZ, NY), 1.0, 6.0, ((0, 16), (1, 2), (3, 8)), jnp.float32)
    observations = centred(key_list[1], (NX, NY), 1.0, 6.0, ((0, 8),), jnp.float32)
    obs_precision = jnp.clip(jnp.exp(math.log(0.02) - 2.30258502 * jax.random.uniform(key_list[2], (NX, NY), jnp.float32) ** steps_of(key_list[2], (NX, NY), ((0, 8),), -0.2, 0.2)), 0.002, 0.02)
    island_ancestor = draw_island_ancestor(jax.random.fold_in(key_list[5], 71), 0)
    particle_ancestor = draw_particle_ancestor(jax.random.fold_in(key_list[5], 71), 0)
    return dict(ensemble=ensemble, observations=observations, obs_precision=obs_precision, island_ancestor=island_ancestor, particle_ancestor=particle_ancestor)


dt_step = 0.2
viscosity = 0.05
stratification = 1.0
relaxation = 0.8


def pad_east(field, width):
    pad_widths = [(0, 0)] * field.ndim
    pad_widths[-3] = (width, width)
    return jnp.pad(field, pad_widths, mode="wrap")


def pad_vertical(field, width):
    pad_widths = [(0, 0)] * field.ndim
    pad_widths[-2] = (width, width)
    return jnp.pad(field, pad_widths)


def fourth_north(field):
    return (8.0 * (jnp.roll(field, -1, -1) - jnp.roll(field, 1, -1)) - (jnp.roll(field, -2, -1) - jnp.roll(field, 2, -1))) / 12.0


def fourth_vertical(field):
    padded = pad_vertical(field, 2)
    return (8.0 * (padded[..., 3:-1, :] - padded[..., 1:-3, :]) - (padded[..., 4:, :] - padded[..., :-4, :])) / 12.0


def fourth_east(extended):
    return (8.0 * (extended[..., 3:-1, :, :] - extended[..., 1:-3, :, :]) - (extended[..., 4:, :, :] - extended[..., :-4, :, :])) / 12.0


def second_north(field):
    return 0.5 * (jnp.roll(field, -1, -1) - jnp.roll(field, 1, -1))


def second_vertical(field):
    padded = pad_vertical(field, 1)
    return 0.5 * (padded[..., 2:, :] - padded[..., :-2, :])


def centred_east(padded):
    return 0.5 * (padded[..., 2:, :, :] - padded[..., :-2, :, :])


def neighbours(padded):
    middle = padded[..., 1:-1, :, :]
    vertical = pad_vertical(middle, 1)
    return (padded[..., 2:, :, :] + padded[..., :-2, :, :] + jnp.roll(middle, 1, -1) + jnp.roll(middle, -1, -1)
            + vertical[..., 2:, :] + vertical[..., :-2, :])


def tendency(extended, zonal, merid, vertical_flow):
    field = extended[..., 2:-2, :, :]
    laplace = neighbours(extended[..., 1:-1, :, :]) - 6.0 * field
    advect = zonal * fourth_east(extended) + merid * fourth_north(field) + vertical_flow * fourth_vertical(field)
    return viscosity * laplace - advect


def sweep(padded, divergence):
    middle = padded[..., 1:-1, :, :]
    return middle + relaxation * (neighbours(padded) - 6.0 * middle - divergence) / 6.0


def log_total(values, axis_index):
    upper_boundary = jnp.max(values, axis=axis_index, keepdims=True)
    return jnp.squeeze(upper_boundary, axis_index) + jnp.log(jnp.sum(jnp.exp(values - upper_boundary), axis=axis_index))


def advance_island_members(model_state):
    zonal = model_state[:, 0]
    merid = model_state[:, 1]
    vertical_flow = model_state[:, 2]
    buoyancy = model_state[:, 3]
    extended = pad_east(model_state, 2)
    star_zonal = zonal + dt_step * tendency(extended[:, 0], zonal, merid, vertical_flow)
    star_merid = merid + dt_step * tendency(extended[:, 1], zonal, merid, vertical_flow)
    star_vertical = vertical_flow + dt_step * (tendency(extended[:, 2], zonal, merid, vertical_flow) + buoyancy)
    buoyancy_provisional_tendency = buoyancy + dt_step * (tendency(extended[:, 3], zonal, merid, vertical_flow) - stratification * vertical_flow)
    divergence = centred_east(pad_east(star_zonal, 1)) + second_north(star_merid) + second_vertical(star_vertical)
    potential = -relaxation * divergence / 6.0
    for repeat_index in range(SWEEPS):
        potential = sweep(pad_east(potential, 1), divergence)
    padded = pad_east(potential, 1)
    return jnp.stack([star_zonal - centred_east(padded), star_merid - second_north(potential),
                      star_vertical - second_vertical(potential), buoyancy_provisional_tendency], axis=1)


def reference(ensemble, observations, obs_precision, island_ancestor, particle_ancestor):
    advance_ensemble = lax.map(advance_island_members, ensemble)
    upper_boundary = advance_ensemble[:, :, 3, :, -1, :]
    ramp = 1.0 + jnp.arange(NX, dtype=jnp.float32) * (2.0 / (NX - 1))
    scale = obs_precision * ramp[:, None]
    misfit = jnp.sum((upper_boundary - observations) ** 2 * scale, axis=(2, 3))
    log_weight = -0.5 * misfit
    island_total = log_total(log_weight, 1)
    particle_logw = log_weight - island_total[:, None]
    island_logw = island_total - log_total(island_total, 0)
    resampled = advance_ensemble[island_ancestor[:, None], particle_ancestor]
    return resampled, particle_logw, island_logw
```

```python
import functools
import jax
import jax.numpy as jnp
from jax import lax
from jax.experimental import pallas as pl
from jax.experimental.pallas import tpu as pltpu
from jax.sharding import PartitionSpec as P

SWEEPS = 8


dt_step = 0.2
viscosity = 0.05
stratification = 1.0
relaxation = 0.8


def extended_2(cells, sides, width):
    for axis, dim in sides:
        count = lax.axis_size(axis)
        head = lax.slice_in_dim(cells, 0, width, axis=dim)
        tail = lax.slice_in_dim(cells, cells.shape[dim] - width, cells.shape[dim], axis=dim)
        cells = jnp.concatenate(
            [
                lax.ppermute(tail, axis, [(i, (i + 1) % count) for i in range(count)]),
                cells,
                lax.ppermute(head, axis, [((i + 1) % count, i) for i in range(count)]),
            ],
            axis=dim,
        )
    return cells


def pad_vertical(field, width):
    pad_widths = [(0, 0)] * field.ndim
    pad_widths[-2] = (width, width)
    return jnp.pad(field, pad_widths)


def fourth_north(field):
    return (
        8.0 * (jnp.roll(field, -1, -1) - jnp.roll(field, 1, -1))
        - (jnp.roll(field, -2, -1) - jnp.roll(field, 2, -1))
    ) / 12.0


def fourth_vertical(field):
    padded = pad_vertical(field, 2)
    return (
        8.0 * (padded[..., 3:-1, :] - padded[..., 1:-3, :])
        - (padded[..., 4:, :] - padded[..., :-4, :])
    ) / 12.0


def fourth_east(extended):
    return (
        8.0 * (extended[..., 3:-1, :, :] - extended[..., 1:-3, :, :])
        - (extended[..., 4:, :, :] - extended[..., :-4, :, :])
    ) / 12.0


def second_north(field):
    return 0.5 * (jnp.roll(field, -1, -1) - jnp.roll(field, 1, -1))


def second_vertical(field):
    padded = pad_vertical(field, 1)
    return 0.5 * (padded[..., 2:, :] - padded[..., :-2, :])


def centred_east(padded):
    return 0.5 * (padded[..., 2:, :, :] - padded[..., :-2, :, :])


def neighbours(padded):
    middle = padded[..., 1:-1, :, :]
    vertical = pad_vertical(middle, 1)
    return (
        padded[..., 2:, :, :]
        + padded[..., :-2, :, :]
        + jnp.roll(middle, 1, -1)
        + jnp.roll(middle, -1, -1)
        + vertical[..., 2:, :]
        + vertical[..., :-2, :]
    )


def tendency(extended, zonal, merid, vertical_flow):
    field = extended[..., 2:-2, :, :]
    laplace = neighbours(extended[..., 1:-1, :, :]) - 6.0 * field
    advect = (
        zonal * fourth_east(extended)
        + merid * fourth_north(field)
        + vertical_flow * fourth_vertical(field)
    )
    return viscosity * laplace - advect


def sweep(padded, divergence):
    middle = padded[..., 1:-1, :, :]
    return middle + relaxation * (neighbours(padded) - 6.0 * middle - divergence) / 6.0


MESH = pl.DeviceIdType.MESH
NPEER = 32
GROUPS = ((0, 1), (1, 1), (2, 1), (3, 1))


def place_of(flat):
    return {"isl": flat % 16, "par": flat // 16}


def peer_of(me, k):
    z = (me // 4 + k // 4) % 8
    x = (me % 4 + k % 4) % 4
    return z * 4 + x


def chunk_of(ref, first, count, flat):
    row = flat // 8
    level = pl.multiple_of((flat // 2) % 4 * 8, 8)
    lane = pl.multiple_of(flat % 2 * 256, 256)
    return ref.at[pl.ds(first, count), row, pl.ds(level, 8), pl.ds(lane, 256)]


def route_kernel(anc, field, part, pick, out, logp, logi, *scratch):
    ng = len(GROUPS)
    held = scratch[:ng]
    sent = scratch[ng : 2 * ng]
    picks, parts, totals, s1, r1, s2, r2, ssem, rsem = scratch[2 * ng :]
    isl = lax.axis_index("isl")
    par = lax.axis_index("par")
    sp = lax.axis_index("sp")
    me = par * 16 + isl
    barrier = pltpu.get_barrier_semaphore()

    @pl.loop(1, NPEER)
    def _(k):
        pl.semaphore_signal(barrier, inc=1, device_id=place_of(peer_of(me, k)), device_id_type=MESH)

    @pl.loop(1, 8)
    def _(k):
        pl.semaphore_signal(barrier, inc=1, device_id={"sp": (sp + k) % 8}, device_id_type=MESH)

    pl.semaphore_wait(barrier, NPEER - 1 + 7)

    def small(src, dst, sem, where):
        return pltpu.make_async_remote_copy(
            src_ref=src, dst_ref=dst, send_sem=ssem.at[sem], recv_sem=rsem.at[sem], device_id=where, device_id_type=MESH
        )

    picks[me] = pick[...]
    parts[sp] = part[...]

    @pl.loop(1, NPEER)
    def _(k):
        small(pick, picks.at[me], 0, place_of(peer_of(me, k))).start()

    @pl.loop(1, 8)
    def _(k):
        small(part, parts.at[sp], 1, {"sp": (sp + k) % 8}).start()

    def first_copy(g, to):
        f0, n = GROUPS[g]
        return pltpu.make_async_remote_copy(
            src_ref=chunk_of(field, f0, n, to), dst_ref=held[g].at[me], send_sem=s1.at[g], recv_sem=r1.at[g],
            device_id=place_of(to), device_id_type=MESH)

    def second_copy(g, to):
        f0, n = GROUPS[g]
        return pltpu.make_async_remote_copy(
            src_ref=sent[g].at[to], dst_ref=chunk_of(out, f0, n, me), send_sem=s2.at[g], recv_sem=r2.at[g],
            device_id=place_of(to), device_id_type=MESH)

    def all_of(g, s, r):
        return pltpu.make_async_remote_copy(
            src_ref=sent[g].at[pl.ds(0, NPEER - 1)], dst_ref=held[g].at[pl.ds(0, NPEER - 1)], send_sem=s.at[g],
            recv_sem=r.at[g], device_id={"sp": (sp + 1) % 8}, device_id_type=MESH)

    for g in range(ng):
        f0, n = GROUPS[g]
        held[g][me] = chunk_of(field, f0, n, me)[...]

        @pl.loop(1, NPEER)
        def _(k):
            first_copy(g, peer_of(me, k)).start()

    small(parts.at[pl.ds(0, 7)], parts.at[pl.ds(0, 7)], 1, {"sp": (sp + 1) % 8}).wait()
    mis = parts[0]
    for k in range(1, 8):
        mis = mis + parts[k]
    totals[me] = -0.5 * mis

    @pl.loop(1, NPEER)
    def _(k):
        small(totals.at[me], totals.at[me], 2, place_of(peer_of(me, k))).start()

    small(picks.at[pl.ds(0, NPEER - 1)], picks.at[pl.ds(0, NPEER - 1)], 0, {"sp": (sp + 1) % 8}).wait()

    for g in range(ng):
        f0, n = GROUPS[g]
        all_of(g, s1, r1).wait_recv()

        @pl.loop(0, NPEER)
        def _(d):
            src = anc[d % 16]
            choose = jnp.broadcast_to(picks[d][None], (n, 8, 128))
            for h in range(2):
                lo = held[g][src, :, :, h * 128 : (h + 1) * 128]
                hi = held[g][src + 16, :, :, h * 128 : (h + 1) * 128]
                sent[g][d, :, :, h * 128 : (h + 1) * 128] = jnp.where(choose < 0.5, lo, hi)

        @pl.loop(1, NPEER)
        def _(k):
            second_copy(g, peer_of(me, k)).start()

        chunk_of(out, f0, n, me)[...] = sent[g][me]

    small(totals.at[pl.ds(0, NPEER - 1)], totals.at[pl.ds(0, NPEER - 1)], 2, {"sp": (sp + 1) % 8}).wait()
    a = totals[0:16]
    b = totals[16:32]
    top = jnp.maximum(a, b)
    isle = top + jnp.log(jnp.exp(a - top) + jnp.exp(b - top))
    peak = jnp.max(isle, axis=0)
    whole = peak + jnp.log(jnp.sum(jnp.exp(isle - peak[None]), axis=0))
    a1 = totals[isl]
    b1 = totals[isl + 16]
    top1 = jnp.maximum(a1, b1)
    mine = top1 + jnp.log(jnp.exp(a1 - top1) + jnp.exp(b1 - top1))
    logp[...] = totals[me] - mine
    logi[...] = mine - whole

    for g in range(ng):
        all_of(g, s1, r1).wait_send()
        all_of(g, s2, r2).wait()


def route(anc, field, part, pick):
    vmem = pl.BlockSpec(memory_space=pltpu.VMEM)
    smem = pl.BlockSpec(memory_space=pltpu.SMEM)
    bufs = [pltpu.VMEM((NPEER, n, 8, 256), jnp.float32) for _, n in GROUPS]
    ng = len(GROUPS)
    return pl.pallas_call(
        route_kernel,
        out_shape=(
            jax.ShapeDtypeStruct(field.shape, jnp.float32),
            jax.ShapeDtypeStruct((1, 128), jnp.float32),
            jax.ShapeDtypeStruct((1, 128), jnp.float32),
        ),
        in_specs=[smem, vmem, vmem, vmem],
        out_specs=(vmem, vmem, vmem),
        scratch_shapes=bufs + bufs + [
            pltpu.VMEM((NPEER, 1, 128), jnp.float32),
            pltpu.VMEM((8, 1, 128), jnp.float32),
            pltpu.VMEM((NPEER, 1, 128), jnp.float32),
            pltpu.SemaphoreType.DMA((ng,)),
            pltpu.SemaphoreType.DMA((ng,)),
            pltpu.SemaphoreType.DMA((ng,)),
            pltpu.SemaphoreType.DMA((ng,)),
            pltpu.SemaphoreType.DMA((3,)),
            pltpu.SemaphoreType.DMA((3,)),
        ],
        compiler_params=pltpu.CompilerParams(collective_id=0, has_side_effects=True),
    )(anc, field, part, pick)


def shards(ensemble, observations, obs_precision, island_ancestor, particle_ancestor):
    model_state = ensemble[0]
    rows_east = model_state.shape[2]
    picks = particle_ancestor[0]
    zonal = model_state[:, 0]
    merid = model_state[:, 1]
    vertical_flow = model_state[:, 2]
    buoyancy = model_state[:, 3]
    extended = extended_2(model_state, (("sp", 2),), 2)
    star_zonal = zonal + dt_step * tendency(extended[:, 0], zonal, merid, vertical_flow)
    star_merid = merid + dt_step * tendency(extended[:, 1], zonal, merid, vertical_flow)
    star_vertical = vertical_flow + dt_step * (
        tendency(extended[:, 2], zonal, merid, vertical_flow) + buoyancy
    )
    buoyancy_provisional_tendency = buoyancy + dt_step * (
        tendency(extended[:, 3], zonal, merid, vertical_flow) - stratification * vertical_flow
    )
    zonal_wide = extended_2(star_zonal, (("sp", 1),), 1)
    divergence = (
        centred_east(zonal_wide) + second_north(star_merid) + second_vertical(star_vertical)
    )
    potential = -relaxation * divergence / 6.0
    for repeat_index in range(SWEEPS):
        padded = extended_2(potential, (("sp", 1),), 1)
        potential = sweep(padded, divergence)
    padded = extended_2(potential, (("sp", 1),), 1)
    stepped = jnp.stack(
        [
            star_zonal - centred_east(padded),
            star_merid - second_north(potential),
            star_vertical - second_vertical(potential),
            buoyancy_provisional_tendency,
        ],
        axis=1,
    )
    upper_boundary = stepped[:, 3][:, :, -1, :]
    nx_total = lax.axis_size("sp") * rows_east
    positions = (lax.axis_index("sp") * rows_east + jnp.arange(rows_east, dtype=jnp.int32)).astype(
        jnp.float32
    )
    ramp = 1.0 + positions * (2.0 / (nx_total - 1))
    scale = obs_precision * ramp[:, None]
    partial_value = jnp.sum((upper_boundary - observations) ** 2 * scale, axis=(1, 2))
    part = jnp.broadcast_to(partial_value[:, None], (1, 128))
    pick = jnp.broadcast_to(picks[:, None].astype(jnp.float32), (1, 128))
    out, logp, logi = route(island_ancestor, stepped[0], part, pick)
    return (out[None, None], logp[:, :1], logi[0, :1])


def solution(mesh):
    return jax.shard_map(
        shards,
        mesh=mesh,
        in_specs=(
            P("isl", "par", None, "sp", None, None),
            P("sp", None),
            P("sp", None),
            P(),
            P("isl", "par"),
        ),
        out_specs=(P("isl", "par", None, "sp", None, None), P("isl", "par"), P("isl")),
        check_vma=False,
    )
```

```python
import jax
import jax.numpy as jnp
from jax import lax
from jax.experimental import pallas as pl
from jax.experimental.pallas import tpu as pltpu
from jax.sharding import PartitionSpec as P

MESH = pl.DeviceIdType.MESH
NPEER = 32
ORDER = (3, 0, 1, 2)
STEP = 0.2
VISC = 0.05
STRAT = 1.0
RELAX = 0.8
Z0 = 8
NZ = 32
LANES = 512


def place_of(flat):
    return {"isl": flat % 16, "par": flat // 16}


def peer_of(me, k):
    z = (me // 4 + k // 4) % 8
    x = (me % 4 + k % 4) % 4
    return z * 4 + x


def chunk_of(ref, flat):
    row = flat // 8
    level = pl.multiple_of((flat // 2) % 4 * 8, 8)
    lane = pl.multiple_of(flat % 2 * 256, 256)
    return ref.at[row, pl.ds(level, 8), pl.ds(lane, 256)]


def north(q, k):
    return pltpu.roll(q, k % LANES, 1)


def pad_rows(ref, rows):
    zero = jnp.zeros((8, LANES), jnp.float32)

    @pl.loop(0, rows)
    def _(r):
        ref[r, 0:Z0, :] = zero
        ref[r, Z0 + NZ : Z0 + NZ + 8, :] = zero


def kernel(
    anc, pick, obs, prec, ens, out, logp, logi,
    xu, xv, xw, xb, su, sv, sw, dv, pa, pb, p3, p6, fore,
    h0, h1, h2, h3, g0, g1, g2, g3, picks, parts, totals,
    lsem, hs, hr, s1, r1, s2, r2, ssem, rsem,
):
    held = (h0, h1, h2, h3)
    sent = (g0, g1, g2, g3)
    isl = lax.axis_index("isl")
    par = lax.axis_index("par")
    sp = lax.axis_index("sp")
    me = par * 16 + isl
    after = {"sp": (sp + 1) % 8}
    before = {"sp": (sp + 7) % 8}
    fields = (xu, xv, xw, xb)
    barrier = pltpu.get_barrier_semaphore()

    @pl.loop(1, NPEER)
    def _(k):
        pl.semaphore_signal(barrier, inc=1, device_id=place_of(peer_of(me, k)), device_id_type=MESH)

    @pl.loop(1, 8)
    def _(k):
        pl.semaphore_signal(barrier, inc=1, device_id={"sp": (sp + k) % 8}, device_id_type=MESH)

    loads = [
        pltpu.make_async_copy(ens.at[f], fields[f].at[3:7, Z0 : Z0 + NZ, :], lsem.at[f]) for f in range(4)
    ]
    for load in loads:
        load.start()

    def remote(src, dst, ss, rs, where):
        return pltpu.make_async_remote_copy(
            src_ref=src, dst_ref=dst, send_sem=ss, recv_sem=rs, device_id=where, device_id_type=MESH
        )

    def small(src, dst, sem, where):
        return remote(src, dst, ssem.at[sem], rsem.at[sem], where)

    pad_rows(xu, 10)
    pad_rows(xv, 10)
    pad_rows(xw, 10)
    pad_rows(xb, 10)
    pad_rows(sw, 4)
    pad_rows(dv, 10)
    pad_rows(pa, 8)
    pad_rows(pb, 6)
    pad_rows(p3, 10)
    pad_rows(p6, 10)
    picks[me] = jnp.full((1, 128), pick[0, 0], jnp.int32).astype(jnp.float32)

    pl.semaphore_wait(barrier, NPEER - 1 + 7)

    edges = []
    for f in range(4):
        w = 3 if f == 0 else 2
        to_after = remote(
            ens.at[f, 4 - w : 4], fields[f].at[3 - w : 3, Z0 : Z0 + NZ, :], hs.at[f, 0], hr.at[f, 0], after
        )
        to_before = remote(
            ens.at[f, 0:w], fields[f].at[7 : 7 + w, Z0 : Z0 + NZ, :], hs.at[f, 1], hr.at[f, 1], before
        )
        edges += [to_after, to_before]
    for edge in edges:
        edge.start()

    @pl.loop(1, NPEER)
    def _(k):
        small(picks.at[me], picks.at[me], 0, place_of(peer_of(me, k))).start()

    for load in loads:
        load.wait()
    for edge in edges:
        edge.wait()

    def tendency(q, r, zb, u, v, w):
        s = Z0 + 8 * zb
        c = q[r, s : s + 8, :]
        xp = q[r + 1, s : s + 8, :]
        xm = q[r - 1, s : s + 8, :]
        xpp = q[r + 2, s : s + 8, :]
        xmm = q[r - 2, s : s + 8, :]
        zp = q[r, s + 1 : s + 9, :]
        zm = q[r, s - 1 : s + 7, :]
        zpp = q[r, s + 2 : s + 10, :]
        zmm = q[r, s - 2 : s + 6, :]
        yp = north(c, -1)
        ym = north(c, 1)
        ypp = north(c, -2)
        ymm = north(c, 2)
        lap = (xp + xm) + (yp + ym) + (zp + zm) - 6.0 * c
        adv = (
            u * (8.0 * (xp - xm) - (xpp - xmm))
            + v * (8.0 * (yp - ym) - (ypp - ymm))
            + w * (8.0 * (zp - zm) - (zpp - zmm))
        )
        return c, (STEP * VISC) * lap - adv

    def winds(r, zb):
        s = Z0 + 8 * zb
        return tuple(q[r, s : s + 8, :] * (STEP / 12.0) for q in (xu, xv, xw))

    @pl.loop(0, 4)
    def _(i):
        r = i + 3
        for zb in range(4):
            s = 8 * zb
            u, v, w = winds(r, zb)
            c, g = tendency(xb, r, zb, u, v, w)
            flow = xw[r, Z0 + s : Z0 + s + 8, :]
            fore[3, i, s : s + 8, :] = c + g - (STEP * STRAT) * flow

    acc = jnp.zeros((1, LANES), jnp.float32)
    for i in range(4):
        gap = fore[3, i, NZ - 1 : NZ, :] - obs[i : i + 1, :]
        ramp = 1.0 + (sp * 4 + i).astype(jnp.float32) * (2.0 / 31.0)
        acc = acc + gap * gap * (prec[i : i + 1, :] * ramp)
    parts[sp] = jnp.broadcast_to(jnp.sum(acc, axis=1, keepdims=True), (1, 128))

    def first_copy(g, to):
        return remote(chunk_of(fore.at[g], to), held[g].at[me], s1.at[g], r1.at[g], place_of(to))

    def second_copy(g, to):
        return remote(sent[g].at[to], chunk_of(out.at[g], me), s2.at[g], r2.at[g], place_of(to))

    def all_of(g, s, r):
        return remote(
            sent[g].at[pl.ds(0, NPEER - 1)], held[g].at[pl.ds(0, NPEER - 1)], s.at[g], r.at[g], after
        )

    def start_first(g):
        held[g][me] = chunk_of(fore.at[g], me)[...]

        @pl.loop(1, NPEER)
        def _(k):
            first_copy(g, peer_of(me, k)).start()

    def start_second(g):
        all_of(g, s1, r1).wait_recv()

        @pl.loop(0, NPEER)
        def _(d):
            src = anc[d % 16]
            choose = jnp.broadcast_to(picks[d], (8, 128)) < 0.5
            for h in range(2):
                lo = held[g][src, :, h * 128 : (h + 1) * 128]
                hi = held[g][src + 16, :, h * 128 : (h + 1) * 128]
                sent[g][d, :, h * 128 : (h + 1) * 128] = jnp.where(choose, lo, hi)

        @pl.loop(1, NPEER)
        def _(k):
            second_copy(g, peer_of(me, k)).start()

        chunk_of(out.at[g], me)[...] = sent[g][me]

    start_first(3)

    @pl.loop(1, 8)
    def _(k):
        small(parts.at[sp], parts.at[sp], 1, {"sp": (sp + k) % 8}).start()

    @pl.loop(0, 6)
    def _(i):
        r = i + 2
        for zb in range(4):
            s = 8 * zb
            u, v, w = winds(r, zb)
            c, g = tendency(xu, r, zb, u, v, w)
            su[i, s : s + 8, :] = c + g

    @pl.loop(0, 4)
    def _(i):
        r = i + 3
        for zb in range(4):
            s = 8 * zb
            u, v, w = winds(r, zb)
            c, g = tendency(xv, r, zb, u, v, w)
            star = c + g
            sv[i, s : s + 8, :] = star
            dv[r, Z0 + s : Z0 + s + 8, :] = 0.5 * (north(star, -1) - north(star, 1))
            c, g = tendency(xw, r, zb, u, v, w)
            sw[i, Z0 + s : Z0 + s + 8, :] = c + g + STEP * xb[r, Z0 + s : Z0 + s + 8, :]

    @pl.loop(0, 4)
    def _(i):
        for zb in range(4):
            s = 8 * zb
            t = Z0 + s
            dx = 0.5 * (su[i + 2, s : s + 8, :] - su[i, s : s + 8, :])
            dz = 0.5 * (sw[i, t + 1 : t + 9, :] - sw[i, t - 1 : t + 7, :])
            dv[i + 3, t : t + 8, :] = dx + dv[i + 3, t : t + 8, :] + dz

    def exchange(buf, e):
        copies = (
            remote(buf.at[4:7, Z0 : Z0 + NZ, :], buf.at[0:3, Z0 : Z0 + NZ, :], hs.at[e, 0], hr.at[e, 0], after),
            remote(buf.at[3:6, Z0 : Z0 + NZ, :], buf.at[7:10, Z0 : Z0 + NZ, :], hs.at[e, 1], hr.at[e, 1], before),
        )
        for copy in copies:
            copy.start()
        return copies

    def finish(copies):
        for copy in copies:
            copy.wait()

    def sweep(src, dst, count, dst0, div0, first=False):
        @pl.loop(0, count)
        def _(i):
            for zb in range(4):
                t = Z0 + 8 * zb
                c = src[i + 1, t : t + 8, :]
                near = (
                    (src[i + 2, t : t + 8, :] + src[i, t : t + 8, :])
                    + (north(c, 1) + north(c, -1))
                    + (src[i + 1, t + 1 : t + 9, :] + src[i + 1, t - 1 : t + 7, :])
                )
                if first:
                    k = -RELAX / 6.0
                    val = (k * (1.0 - RELAX) - RELAX / 6.0) * c + (k * RELAX / 6.0) * near
                else:
                    d = dv[i + div0, t : t + 8, :]
                    val = (1.0 - RELAX) * c + (RELAX / 6.0) * (near - d)
                dst[i + dst0, t : t + 8, :] = val

    finish(exchange(dv, 4))
    sweep(dv, pa, 8, 0, 1, first=True)
    sweep(pa, pb, 6, 0, 2)
    sweep(pb, p3, 4, 3, 3)
    moving = exchange(p3, 5)

    small(parts.at[pl.ds(0, 7)], parts.at[pl.ds(0, 7)], 1, after).wait()
    mis = parts[0]
    for k in range(1, 8):
        mis = mis + parts[k]
    totals[me] = -0.5 * mis

    @pl.loop(1, NPEER)
    def _(k):
        small(totals.at[me], totals.at[me], 2, place_of(peer_of(me, k))).start()

    finish(moving)
    sweep(p3, pa, 8, 0, 1)
    sweep(pa, pb, 6, 0, 2)
    sweep(pb, p6, 4, 3, 3)
    moving = exchange(p6, 6)

    small(picks.at[pl.ds(0, NPEER - 1)], picks.at[pl.ds(0, NPEER - 1)], 0, after).wait()
    start_second(3)

    finish(moving)
    sweep(p6, pa, 8, 0, 1)
    sweep(pa, pb, 6, 0, 2)

    @pl.loop(0, 4)
    def _(i):
        for zb in range(4):
            s = 8 * zb
            t = Z0 + s
            fore[0, i, s : s + 8, :] = su[i + 1, s : s + 8, :] - 0.5 * (
                pb[i + 2, t : t + 8, :] - pb[i, t : t + 8, :]
            )

    start_first(0)

    @pl.loop(0, 4)
    def _(i):
        for zb in range(4):
            s = 8 * zb
            t = Z0 + s
            c = pb[i + 1, t : t + 8, :]
            fore[1, i, s : s + 8, :] = sv[i, s : s + 8, :] - 0.5 * (north(c, -1) - north(c, 1))
            fore[2, i, s : s + 8, :] = sw[i, t : t + 8, :] - 0.5 * (
                pb[i + 1, t + 1 : t + 9, :] - pb[i + 1, t - 1 : t + 7, :]
            )

    start_first(1)
    start_first(2)

    small(totals.at[pl.ds(0, NPEER - 1)], totals.at[pl.ds(0, NPEER - 1)], 2, after).wait()
    a = totals[0:16]
    b = totals[16:32]
    top = jnp.maximum(a, b)
    isle = top + jnp.log(jnp.exp(a - top) + jnp.exp(b - top))
    peak = jnp.max(isle, axis=0)
    whole = peak + jnp.log(jnp.sum(jnp.exp(isle - peak[None]), axis=0))
    a1 = totals[isl]
    b1 = totals[isl + 16]
    top1 = jnp.maximum(a1, b1)
    mine = top1 + jnp.log(jnp.exp(a1 - top1) + jnp.exp(b1 - top1))
    logp[...] = totals[me] - mine
    logi[...] = mine - whole

    for g in range(3):
        start_second(g)
    for g in range(4):
        all_of(g, s1, r1).wait_send()
        all_of(g, s2, r2).wait()


def step(ensemble, observations, obs_precision, island_ancestor, particle_ancestor):
    field = ensemble[0, 0]
    vmem = pl.BlockSpec(memory_space=pltpu.VMEM)
    smem = pl.BlockSpec(memory_space=pltpu.SMEM)
    f32 = jnp.float32
    tall = Z0 + NZ + 8
    dma = pltpu.SemaphoreType.DMA
    out, logp, logi = pl.pallas_call(
        kernel,
        out_shape=(
            jax.ShapeDtypeStruct(field.shape, f32),
            jax.ShapeDtypeStruct((1, 128), f32),
            jax.ShapeDtypeStruct((1, 128), f32),
        ),
        in_specs=[smem, smem, vmem, vmem, pl.BlockSpec(memory_space=pl.ANY)],
        out_specs=(vmem, vmem, vmem),
        scratch_shapes=[pltpu.VMEM((10, tall, LANES), f32) for _ in range(4)]
        + [
            pltpu.VMEM((6, NZ, LANES), f32),
            pltpu.VMEM((4, NZ, LANES), f32),
            pltpu.VMEM((4, tall, LANES), f32),
            pltpu.VMEM((10, tall, LANES), f32),
            pltpu.VMEM((8, tall, LANES), f32),
            pltpu.VMEM((6, tall, LANES), f32),
            pltpu.VMEM((10, tall, LANES), f32),
            pltpu.VMEM((10, tall, LANES), f32),
            pltpu.VMEM((4, 4, NZ, LANES), f32),
        ]
        + [pltpu.VMEM((NPEER, 8, 256), f32) for _ in range(8)]
        + [
            pltpu.VMEM((NPEER, 1, 128), f32),
            pltpu.VMEM((8, 1, 128), f32),
            pltpu.VMEM((NPEER, 1, 128), f32),
            dma((4,)),
            dma((7, 2)),
            dma((7, 2)),
            dma((4,)),
            dma((4,)),
            dma((4,)),
            dma((4,)),
            dma((3,)),
            dma((3,)),
        ],
        compiler_params=pltpu.CompilerParams(
            collective_id=0, has_side_effects=True, vmem_limit_bytes=56 * 1024 * 1024
        ),
    )(island_ancestor, particle_ancestor, observations, obs_precision, field)
    return out[None, None], logp[:, :1], logi[0, :1]


def solution(mesh):
    return jax.shard_map(
        step,
        mesh=mesh,
        in_specs=(
            P("isl", "par", None, "sp", None, None),
            P("sp", None),
            P("sp", None),
            P(),
            P("isl", "par"),
        ),
        out_specs=(P("isl", "par", None, "sp", None, None), P("isl", "par"), P("isl")),
        check_vma=False,
    )
```

```python
import jax
import jax.numpy as jnp
from jax import lax
from jax.experimental import pallas as pl
from jax.experimental.pallas import tpu as pltpu
from jax.sharding import PartitionSpec as P

MESH = pl.DeviceIdType.MESH
NPEER = 32
GROUPS = ((3, 1), (1, 2), (0, 1))
STEP = 0.2
VISC = 0.05
STRAT = 1.0
RELAX = 0.8
Z0 = 8
NZ = 32
LANES = 512


def north(q, k):
    return pltpu.roll(q, k % LANES, 1)


def pad_rows(ref, rows):
    zero = jnp.zeros((8, LANES), jnp.float32)

    @pl.loop(0, rows)
    def _(r):
        ref[r, 0:Z0, :] = zero
        ref[r, Z0 + NZ : Z0 + NZ + 8, :] = zero


def chunk_of(ref, first, count, flat):
    row = flat // 8
    level = pl.multiple_of((flat // 2) % 4 * 8, 8)
    lane = pl.multiple_of(flat % 2 * 256, 256)
    return ref.at[pl.ds(first, count), row, pl.ds(level, 8), pl.ds(lane, 256)]


def kernel(
    anc, pick, obs, prec, ens, out, logp, logi,
    xu, xv, xw, xb, su, sv, sw, dv, a1, a2, a3, a4, a8, fore,
    h0, h1, h2, g0, g1, g2, picks, parts, totals,
    lsem, hs, hr, ws, wr, s1, r1, s2, r2, ssem, rsem, met,
):
    held = (h0, h1, h2)
    sent = (g0, g1, g2)
    isl = lax.axis_index("isl")
    par = lax.axis_index("par")
    sp = lax.axis_index("sp")
    me = par * 16 + isl
    z = par * 4 + lax.div(isl, 4)
    x = lax.rem(isl, 4)
    after = {"sp": lax.rem(sp + 1, 8)}
    before = {"sp": lax.rem(sp + 7, 8)}
    fields = (xu, xv, xw, xb)

    zs = []
    for dz in range(8):
        zt = lax.rem(z + dz, 8)
        zs.append((zt, lax.rem(zt, 4) * 4, lax.div(zt, 4)))
    xs = [lax.rem(x + dx, 4) for dx in range(4)]

    def away(dz, dx):
        zt, zlo4, hi = zs[dz % 8]
        return {"isl": zlo4 + xs[dx % 4], "par": hi}

    peers = []
    for dz in range(8):
        for dx in range(4):
            if dz or dx:
                peers.append((zs[dz][0] * 4 + xs[dx], away(dz, dx)))
    mates = [{"sp": lax.rem(sp + k, 8)} for k in range(1, 8)]

    def tell(sem, where):
        pl.semaphore_signal(sem, inc=1, device_id=where, device_id_type=MESH)

    barrier = pltpu.get_barrier_semaphore()
    close = (after, before, away(0, 1), away(0, 3), away(1, 0), away(7, 0))
    for where in close:
        tell(barrier, where)

    loads = [
        pltpu.make_async_copy(ens.at[f], fields[f].at[3:7, Z0 : Z0 + NZ, :], lsem.at[f]) for f in range(4)
    ]
    for f in (3, 1, 2, 0):
        loads[f].start()

    def remote(src, dst, ss, rs, where):
        return pltpu.make_async_remote_copy(
            src_ref=src, dst_ref=dst, send_sem=ss, recv_sem=rs, device_id=where, device_id_type=MESH
        )

    def small(src, dst, sem, where):
        return remote(src, dst, ssem.at[sem], rsem.at[sem], where)

    pl.semaphore_wait(barrier, len(close))

    edges = {}
    for f in (3, 1, 2, 0):
        w = 3 if f == 0 else 2
        edges[f] = (
            remote(ens.at[f, 4 - w : 4], fields[f].at[3 - w : 3, Z0 : Z0 + NZ, :], hs.at[f, 0], hr.at[f, 0], after),
            remote(ens.at[f, 0:w], fields[f].at[7 : 7 + w, Z0 : Z0 + NZ, :], hs.at[f, 1], hr.at[f, 1], before),
        )
        for edge in edges[f]:
            edge.start()

    pad_rows(xb, 10)
    pad_rows(xv, 10)
    pad_rows(xw, 10)
    pad_rows(xu, 10)

    for step_, pairs in enumerate(
        (
            (away(1, 0), away(7, 0)),
            (away(2, 0), away(6, 0)),
            (away(0, 1), away(0, 3)),
            (away(0, 1), away(0, 3)),
        )
    ):
        for where in pairs:
            tell(met.at[step_], where)
        if step_ < 2:
            for where in ((after, before), (mates[1], mates[5]))[step_]:
                tell(met.at[4 + step_], where)
        pl.semaphore_wait(met.at[step_], 2)
        if step_ < 2:
            pl.semaphore_wait(met.at[4 + step_], 2)

    picks[me] = jnp.full((1, 128), pick[0, 0], jnp.int32).astype(jnp.float32)
    for _, where in peers:
        small(picks.at[me], picks.at[me], 0, where).start()

    pad_rows(sw, 4)
    for ref in (dv, a1, a2, a3, a4, a8):
        pad_rows(ref, 12)

    def land(copies):
        for copy in copies:
            copy.wait_recv()

    def tendency(q, r, zb, u, v, w):
        s = Z0 + 8 * zb
        c = q[r, s : s + 8, :]
        xp = q[r + 1, s : s + 8, :]
        xm = q[r - 1, s : s + 8, :]
        xpp = q[r + 2, s : s + 8, :]
        xmm = q[r - 2, s : s + 8, :]
        zp = q[r, s + 1 : s + 9, :]
        zm = q[r, s - 1 : s + 7, :]
        zpp = q[r, s + 2 : s + 10, :]
        zmm = q[r, s - 2 : s + 6, :]
        yp = north(c, -1)
        ym = north(c, 1)
        ypp = north(c, -2)
        ymm = north(c, 2)
        lap = (xp + xm) + (yp + ym) + (zp + zm) - 6.0 * c
        adv = (
            u * (8.0 * (xp - xm) - (xpp - xmm))
            + v * (8.0 * (yp - ym) - (ypp - ymm))
            + w * (8.0 * (zp - zm) - (zpp - zmm))
        )
        return c, (STEP * VISC) * lap - adv

    def winds(r, zb):
        s = Z0 + 8 * zb
        return tuple(q[r, s : s + 8, :] * (STEP / 12.0) for q in (xu, xv, xw))

    def first_copy(g, flat, where):
        f, n = GROUPS[g]
        return remote(chunk_of(fore, f, n, flat), held[g].at[me], s1.at[g], r1.at[g], where)

    def second_copy(g, flat, where):
        f, n = GROUPS[g]
        return remote(sent[g].at[flat], chunk_of(out, f, n, me), s2.at[g], r2.at[g], where)

    def all_of(g, s, r):
        return remote(
            sent[g].at[pl.ds(0, NPEER - 1)], held[g].at[pl.ds(0, NPEER - 1)], s.at[g], r.at[g], after
        )

    def start_first(g):
        f, n = GROUPS[g]
        for flat, where in peers:
            first_copy(g, flat, where).start()
        held[g][me] = chunk_of(fore, f, n, me)[...]

    def start_second(g):
        f, n = GROUPS[g]
        all_of(g, s1, r1).wait_recv()

        @pl.loop(0, NPEER)
        def _(d):
            src = anc[lax.rem(d, 16)]
            choose = jnp.broadcast_to(picks[d][None], (n, 8, 128)) < 0.5
            for h in range(2):
                lanes = slice(h * 128, (h + 1) * 128)
                lo = held[g][src, :, :, lanes]
                hi = held[g][src + 16, :, :, lanes]
                sent[g][d, :, :, lanes] = jnp.where(choose, lo, hi)

        for flat, where in peers:
            second_copy(g, flat, where).start()
        chunk_of(out, f, n, me)[...] = sent[g][me]

    for load in loads[:3]:
        load.wait()
    loads[3].wait()
    land(edges[3])

    @pl.loop(0, 4)
    def _(i):
        r = i + 3
        for zb in range(4):
            s = 8 * zb
            u, v, w = winds(r, zb)
            c, g = tendency(xb, r, zb, u, v, w)
            flow = xw[r, Z0 + s : Z0 + s + 8, :]
            fore[3, i, s : s + 8, :] = c + g - (STEP * STRAT) * flow

    start_first(0)

    land(edges[1])

    @pl.loop(0, 4)
    def _(i):
        r = i + 3
        for zb in range(4):
            s = 8 * zb
            u, v, w = winds(r, zb)
            c, g = tendency(xv, r, zb, u, v, w)
            star = c + g
            sv[i, s : s + 8, :] = star
            dv[i + 4, Z0 + s : Z0 + s + 8, :] = 0.5 * (north(star, -1) - north(star, 1))

    land(edges[2])

    @pl.loop(0, 4)
    def _(i):
        r = i + 3
        for zb in range(4):
            s = 8 * zb
            u, v, w = winds(r, zb)
            c, g = tendency(xw, r, zb, u, v, w)
            sw[i, Z0 + s : Z0 + s + 8, :] = c + g + STEP * xb[r, Z0 + s : Z0 + s + 8, :]

    land(edges[0])

    @pl.loop(0, 6)
    def _(i):
        r = i + 2
        for zb in range(4):
            s = 8 * zb
            u, v, w = winds(r, zb)
            c, g = tendency(xu, r, zb, u, v, w)
            su[i, s : s + 8, :] = c + g

    @pl.loop(0, 4)
    def _(i):
        for zb in range(4):
            s = 8 * zb
            t = Z0 + s
            dx = 0.5 * (su[i + 2, s : s + 8, :] - su[i, s : s + 8, :])
            dz = 0.5 * (sw[i, t + 1 : t + 9, :] - sw[i, t - 1 : t + 7, :])
            dv[i + 4, t : t + 8, :] = dx + dv[i + 4, t : t + 8, :] + dz

    def ship(buf, e, away_rows):
        copies = {}
        for j in away_rows:
            copies[j] = (
                remote(
                    buf.at[8 - j, Z0 : Z0 + NZ, :], buf.at[4 - j, Z0 : Z0 + NZ, :], ws.at[e, j, 0], wr.at[e, j, 0], after
                ),
                remote(
                    buf.at[3 + j, Z0 : Z0 + NZ, :], buf.at[7 + j, Z0 : Z0 + NZ, :], ws.at[e, j, 1], wr.at[e, j, 1], before
                ),
            )
            for copy in copies[j]:
                copy.start()
        return copies

    def sweep_row(src, dst, row, first):
        for zb in range(4):
            t = Z0 + 8 * zb
            c = src[row, t : t + 8, :]
            near = (
                (src[row + 1, t : t + 8, :] + src[row - 1, t : t + 8, :])
                + (north(c, 1) + north(c, -1))
                + (src[row, t + 1 : t + 9, :] + src[row, t - 1 : t + 7, :])
            )
            if first:
                k = -RELAX / 6.0
                val = (k * (1.0 - RELAX) - RELAX / 6.0) * c + (k * RELAX / 6.0) * near
            else:
                val = (1.0 - RELAX) * c + (RELAX / 6.0) * (near - dv[row, t : t + 8, :])
            dst[row, t : t + 8, :] = val

    def inner(levels, k, first):
        @pl.loop(0, 2)
        def _(side):
            sweep_row(levels[k - 1], levels[k], 5 + side, first and k == 1)

    def wave(levels, j, first):
        for k in range(1, j + 1):
            d = j - k

            @pl.loop(0, 2)
            def _(side):
                sweep_row(levels[k - 1], levels[k], 4 - d + side * (3 + 2 * d), first and k == 1)

        if j < 4:
            inner(levels, j + 1, first)

    stage = (dv, a1, a2, a3, a4)
    moving = ship(dv, 0, (1, 2, 3, 4))
    inner(stage, 1, True)

    acc = jnp.zeros((1, LANES), jnp.float32)
    for i in range(4):
        gap = fore[3, i, NZ - 1 : NZ, :] - obs[i : i + 1, :]
        ramp = 1.0 + (sp * 4 + i).astype(jnp.float32) * (2.0 / 31.0)
        acc = acc + gap * gap * (prec[i : i + 1, :] * ramp)
    parts[sp] = jnp.broadcast_to(jnp.sum(acc, axis=1, keepdims=True), (1, 128))
    for where in mates:
        small(parts.at[sp], parts.at[sp], 1, where).start()

    for j in (1, 2, 3):
        land(moving[j])
        wave(stage, j, True)
    later = ship(a4, 1, (2, 3))
    land(moving[4])
    wave(stage, 4, True)
    later.update(ship(a4, 1, (1, 4)))

    stage2 = (a4, a1, a2, a3, a8)
    inner(stage2, 1, False)

    small(picks.at[pl.ds(0, NPEER - 1)], picks.at[pl.ds(0, NPEER - 1)], 0, after).wait()
    start_second(0)

    for j in (2, 3, 1):
        land(later[j])
    for j in (1, 2, 3):
        wave(stage2, j, False)
    land(later[4])
    wave(stage2, 4, False)
    last = ship(a8, 2, (1,))

    @pl.loop(0, 4)
    def _(i):
        for zb in range(4):
            s = 8 * zb
            t = Z0 + s
            c = a8[i + 4, t : t + 8, :]
            fore[1, i, s : s + 8, :] = sv[i, s : s + 8, :] - 0.5 * (north(c, -1) - north(c, 1))
            fore[2, i, s : s + 8, :] = sw[i, t : t + 8, :] - 0.5 * (
                a8[i + 4, t + 1 : t + 9, :] - a8[i + 4, t - 1 : t + 7, :]
            )

    start_first(1)

    land(last[1])

    @pl.loop(0, 4)
    def _(i):
        for zb in range(4):
            s = 8 * zb
            t = Z0 + s
            fore[0, i, s : s + 8, :] = su[i + 1, s : s + 8, :] - 0.5 * (
                a8[i + 5, t : t + 8, :] - a8[i + 3, t : t + 8, :]
            )

    start_first(2)

    small(parts.at[pl.ds(0, 7)], parts.at[pl.ds(0, 7)], 1, after).wait()
    mis = parts[0]
    for k in range(1, 8):
        mis = mis + parts[k]
    totals[me] = -0.5 * mis
    for _, where in peers:
        small(totals.at[me], totals.at[me], 2, where).start()

    start_second(1)

    small(totals.at[pl.ds(0, NPEER - 1)], totals.at[pl.ds(0, NPEER - 1)], 2, after).wait()
    a = totals[0:16]
    b = totals[16:32]
    top = jnp.maximum(a, b)
    isle = top + jnp.log(jnp.exp(a - top) + jnp.exp(b - top))
    peak = jnp.max(isle, axis=0)
    whole = peak + jnp.log(jnp.sum(jnp.exp(isle - peak[None]), axis=0))
    own = totals[isl]
    other = totals[isl + 16]
    top1 = jnp.maximum(own, other)
    mine = top1 + jnp.log(jnp.exp(own - top1) + jnp.exp(other - top1))
    logp[...] = totals[me] - mine
    logi[...] = mine - whole

    start_second(2)

    for f in range(4):
        for edge in edges[f]:
            edge.wait_send()
    for group in (moving, later, last):
        for copies in group.values():
            for copy in copies:
                copy.wait_send()
    for g in range(3):
        all_of(g, s1, r1).wait_send()
        all_of(g, s2, r2).wait()


def step(ensemble, observations, obs_precision, island_ancestor, particle_ancestor):
    field = ensemble[0, 0]
    vmem = pl.BlockSpec(memory_space=pltpu.VMEM)
    smem = pl.BlockSpec(memory_space=pltpu.SMEM)
    f32 = jnp.float32
    tall = Z0 + NZ + 8
    dma = pltpu.SemaphoreType.DMA
    out, logp, logi = pl.pallas_call(
        kernel,
        out_shape=(
            jax.ShapeDtypeStruct(field.shape, f32),
            jax.ShapeDtypeStruct((1, 128), f32),
            jax.ShapeDtypeStruct((1, 128), f32),
        ),
        in_specs=[smem, smem, vmem, vmem, pl.BlockSpec(memory_space=pl.ANY)],
        out_specs=(vmem, vmem, vmem),
        scratch_shapes=[pltpu.VMEM((10, tall, LANES), f32) for _ in range(4)]
        + [
            pltpu.VMEM((6, NZ, LANES), f32),
            pltpu.VMEM((4, NZ, LANES), f32),
            pltpu.VMEM((4, tall, LANES), f32),
        ]
        + [pltpu.VMEM((12, tall, LANES), f32) for _ in range(6)]
        + [pltpu.VMEM((4, 4, NZ, LANES), f32)]
        + [pltpu.VMEM((NPEER, n, 8, 256), f32) for _, n in GROUPS + GROUPS]
        + [
            pltpu.VMEM((NPEER, 1, 128), f32),
            pltpu.VMEM((8, 1, 128), f32),
            pltpu.VMEM((NPEER, 1, 128), f32),
            dma((4,)),
            dma((4, 2)),
            dma((4, 2)),
            dma((3, 5, 2)),
            dma((3, 5, 2)),
            dma((3,)),
            dma((3,)),
            dma((3,)),
            dma((3,)),
            dma((3,)),
            dma((3,)),
            pltpu.SemaphoreType.REGULAR((6,)),
        ],
        compiler_params=pltpu.CompilerParams(
            collective_id=0, has_side_effects=True, vmem_limit_bytes=56 * 1024 * 1024
        ),
    )(island_ancestor, particle_ancestor, observations, obs_precision, field)
    return out[None, None], logp[:, :1], logi[0, :1]


def solution(mesh):
    return jax.shard_map(
        step,
        mesh=mesh,
        in_specs=(
            P("isl", "par", None, "sp", None, None),
            P("sp", None),
            P("sp", None),
            P(),
            P("isl", "par"),
        ),
        out_specs=(P("isl", "par", None, "sp", None, None), P("isl", "par"), P("isl")),
        check_vma=False,
    )
```

```python
import jax
import jax.numpy as jnp
from jax import lax
from jax.experimental import pallas as pl
from jax.experimental.pallas import tpu as pltpu
from jax.sharding import PartitionSpec as P

MESH = pl.DeviceIdType.MESH
NPEER = 32
GROUPS = ((3, 1), (1, 2), (0, 1))
STEP = 0.2
VISC = 0.05
STRAT = 1.0
RELAX = 0.8
Z0 = 8
FAR_FIRST = sorted(
    [(dz, dx) for dz in range(8) for dx in range(4) if dz or dx],
    key=lambda k: -(min(k[0], 8 - k[0]) + min(k[1], 4 - k[1])),
)
NZ = 32
LANES = 512


def north(q, k):
    return pltpu.roll(q, k % LANES, 1)


def pad_rows(ref, rows):
    zero = jnp.zeros((8, LANES), jnp.float32)

    @pl.loop(0, rows)
    def _(r):
        ref[r, 0:Z0, :] = zero
        ref[r, Z0 + NZ : Z0 + NZ + 8, :] = zero


def chunk_of(ref, first, count, flat):
    row = flat // 8
    level = pl.multiple_of((flat // 2) % 4 * 8, 8)
    lane = pl.multiple_of(flat % 2 * 256, 256)
    return ref.at[pl.ds(first, count), row, pl.ds(level, 8), pl.ds(lane, 256)]


def kernel(
    anc, pick, obs, prec, ens, out, logp, logi,
    xu, xv, xw, xb, su, sv, sw, dv, a1, a2, a3, a4, a8, fore,
    h0, h1, h2, g0, g1, g2, picks, parts, totals,
    lsem, hs, hr, ws, wr, s1, r1, s2, r2, ssem, rsem, met,
):
    held = (h0, h1, h2)
    sent = (g0, g1, g2)
    isl = lax.axis_index("isl")
    par = lax.axis_index("par")
    sp = lax.axis_index("sp")
    me = par * 16 + isl
    z = par * 4 + lax.div(isl, 4)
    x = lax.rem(isl, 4)
    after = {"sp": lax.rem(sp + 1, 8)}
    before = {"sp": lax.rem(sp + 7, 8)}
    fields = (xu, xv, xw, xb)

    zs = []
    for dz in range(8):
        zt = lax.rem(z + dz, 8)
        zs.append((zt, lax.rem(zt, 4) * 4, lax.div(zt, 4)))
    xs = [lax.rem(x + dx, 4) for dx in range(4)]

    def away(dz, dx):
        zt, zlo4, hi = zs[dz % 8]
        return {"isl": zlo4 + xs[dx % 4], "par": hi}

    peers = []
    for dz, dx in FAR_FIRST:
        peers.append((zs[dz][0] * 4 + xs[dx], away(dz, dx)))
    mates = [{"sp": lax.rem(sp + k, 8)} for k in range(1, 8)]

    def tell(sem, where):
        pl.semaphore_signal(sem, inc=1, device_id=where, device_id_type=MESH)

    barrier = pltpu.get_barrier_semaphore()
    close = (after, before, away(0, 1), away(0, 3), away(1, 0), away(7, 0))
    for where in close:
        tell(barrier, where)

    loads = [
        pltpu.make_async_copy(ens.at[f], fields[f].at[3:7, Z0 : Z0 + NZ, :], lsem.at[f]) for f in range(4)
    ]
    for f in (3, 1, 2, 0):
        loads[f].start()

    def remote(src, dst, ss, rs, where):
        return pltpu.make_async_remote_copy(
            src_ref=src, dst_ref=dst, send_sem=ss, recv_sem=rs, device_id=where, device_id_type=MESH
        )

    def small(src, dst, sem, where):
        return remote(src, dst, ssem.at[sem], rsem.at[sem], where)

    pl.semaphore_wait(barrier, len(close))

    edges = {}
    for f in (3, 1, 2, 0):
        w = 3 if f == 0 else 2
        edges[f] = (
            remote(ens.at[f, 4 - w : 4], fields[f].at[3 - w : 3, Z0 : Z0 + NZ, :], hs.at[f, 0], hr.at[f, 0], after),
            remote(ens.at[f, 0:w], fields[f].at[7 : 7 + w, Z0 : Z0 + NZ, :], hs.at[f, 1], hr.at[f, 1], before),
        )
        for edge in edges[f]:
            edge.start()

    rounds = (
        (away(1, 0), away(7, 0), away(0, 1), away(0, 3), after, before),
        (away(2, 0), away(6, 0), mates[1], mates[5]),
        (away(0, 1), away(0, 3), away(0, 2)),
    )

    def call(k):
        for where in rounds[k]:
            tell(met.at[k], where)

    def hear(k):
        pl.semaphore_wait(met.at[k], len(rounds[k]))

    call(0)
    pad_rows(xb, 10)
    pad_rows(xv, 10)
    pad_rows(xw, 10)
    pad_rows(xu, 10)
    hear(0)
    call(1)
    pad_rows(sw, 4)
    for ref in (dv, a1, a2, a3, a4, a8):
        pad_rows(ref, 12)
    picks[me] = jnp.full((1, 128), pick[0, 0], jnp.int32).astype(jnp.float32)
    hear(1)
    call(2)

    def land(copies):
        for copy in copies:
            copy.wait_recv()

    def tendency(q, r, zb, u, v, w):
        s = Z0 + 8 * zb
        c = q[r, s : s + 8, :]
        xp = q[r + 1, s : s + 8, :]
        xm = q[r - 1, s : s + 8, :]
        xpp = q[r + 2, s : s + 8, :]
        xmm = q[r - 2, s : s + 8, :]
        zp = q[r, s + 1 : s + 9, :]
        zm = q[r, s - 1 : s + 7, :]
        zpp = q[r, s + 2 : s + 10, :]
        zmm = q[r, s - 2 : s + 6, :]
        yp = north(c, -1)
        ym = north(c, 1)
        ypp = north(c, -2)
        ymm = north(c, 2)
        lap = (xp + xm) + (yp + ym) + (zp + zm) - 6.0 * c
        adv = (
            u * (8.0 * (xp - xm) - (xpp - xmm))
            + v * (8.0 * (yp - ym) - (ypp - ymm))
            + w * (8.0 * (zp - zm) - (zpp - zmm))
        )
        return c, (STEP * VISC) * lap - adv

    def put(f, i, zb, value):
        fore[f, i * 8 + zb * 2] = value[:, 0:256]
        fore[f, i * 8 + zb * 2 + 1] = value[:, 256:512]

    def winds(r, zb):
        s = Z0 + 8 * zb
        return tuple(q[r, s : s + 8, :] * (STEP / 12.0) for q in (xu, xv, xw))

    def first_copy(g, flat, where):
        f, n = GROUPS[g]
        return remote(fore.at[pl.ds(f, n), flat], held[g].at[me], s1.at[g], r1.at[g], where)

    def second_copy(g, flat, where):
        f, n = GROUPS[g]
        return remote(sent[g].at[flat], chunk_of(out, f, n, me), s2.at[g], r2.at[g], where)

    def all_of(g, s, r):
        return remote(
            sent[g].at[pl.ds(0, NPEER - 1)], held[g].at[pl.ds(0, NPEER - 1)], s.at[g], r.at[g], after
        )

    def start_first(g):
        f, n = GROUPS[g]
        for flat, where in peers:
            first_copy(g, flat, where).start()
        held[g][me] = fore[pl.ds(f, n), me]

    def start_second(g):
        f, n = GROUPS[g]
        all_of(g, s1, r1).wait_recv()

        @pl.loop(0, NPEER)
        def _(d):
            src = anc[lax.rem(d, 16)]
            choose = jnp.broadcast_to(picks[d][None], (n, 8, 128)) < 0.5
            for h in range(2):
                lanes = slice(h * 128, (h + 1) * 128)
                lo = held[g][src, :, :, lanes]
                hi = held[g][src + 16, :, :, lanes]
                sent[g][d, :, :, lanes] = jnp.where(choose, lo, hi)

        for flat, where in peers:
            second_copy(g, flat, where).start()
        chunk_of(out, f, n, me)[...] = sent[g][me]

    for load in loads[:3]:
        load.wait()
    loads[3].wait()
    land(edges[3])

    @pl.loop(0, 4)
    def _(i):
        r = i + 3
        for zb in range(4):
            s = 8 * zb
            u, v, w = winds(r, zb)
            c, g = tendency(xb, r, zb, u, v, w)
            flow = xw[r, Z0 + s : Z0 + s + 8, :]
            put(3, i, zb, c + g - (STEP * STRAT) * flow)

    hear(2)
    start_first(0)
    for _, where in peers:
        small(picks.at[me], picks.at[me], 0, where).start()

    land(edges[1])

    @pl.loop(0, 4)
    def _(i):
        r = i + 3
        for zb in range(4):
            s = 8 * zb
            u, v, w = winds(r, zb)
            c, g = tendency(xv, r, zb, u, v, w)
            star = c + g
            sv[i, s : s + 8, :] = star
            dv[i + 4, Z0 + s : Z0 + s + 8, :] = 0.5 * (north(star, -1) - north(star, 1))

    land(edges[2])

    @pl.loop(0, 4)
    def _(i):
        r = i + 3
        for zb in range(4):
            s = 8 * zb
            u, v, w = winds(r, zb)
            c, g = tendency(xw, r, zb, u, v, w)
            sw[i, Z0 + s : Z0 + s + 8, :] = c + g + STEP * xb[r, Z0 + s : Z0 + s + 8, :]

    land(edges[0])

    @pl.loop(0, 6)
    def _(i):
        r = i + 2
        for zb in range(4):
            s = 8 * zb
            u, v, w = winds(r, zb)
            c, g = tendency(xu, r, zb, u, v, w)
            su[i, s : s + 8, :] = c + g

    @pl.loop(0, 4)
    def _(i):
        for zb in range(4):
            s = 8 * zb
            t = Z0 + s
            dx = 0.5 * (su[i + 2, s : s + 8, :] - su[i, s : s + 8, :])
            dz = 0.5 * (sw[i, t + 1 : t + 9, :] - sw[i, t - 1 : t + 7, :])
            dv[i + 4, t : t + 8, :] = dx + dv[i + 4, t : t + 8, :] + dz

    def ship(buf, e, away_rows):
        copies = {}
        for j in away_rows:
            copies[j] = (
                remote(
                    buf.at[8 - j, Z0 : Z0 + NZ, :], buf.at[4 - j, Z0 : Z0 + NZ, :], ws.at[e, j, 0], wr.at[e, j, 0], after
                ),
                remote(
                    buf.at[3 + j, Z0 : Z0 + NZ, :], buf.at[7 + j, Z0 : Z0 + NZ, :], ws.at[e, j, 1], wr.at[e, j, 1], before
                ),
            )
            for copy in copies[j]:
                copy.start()
        return copies

    def sweep_row(src, dst, row, first):
        for zb in range(4):
            t = Z0 + 8 * zb
            c = src[row, t : t + 8, :]
            near = (
                (src[row + 1, t : t + 8, :] + src[row - 1, t : t + 8, :])
                + (north(c, 1) + north(c, -1))
                + (src[row, t + 1 : t + 9, :] + src[row, t - 1 : t + 7, :])
            )
            if first:
                k = -RELAX / 6.0
                val = (k * (1.0 - RELAX) - RELAX / 6.0) * c + (k * RELAX / 6.0) * near
            else:
                val = (1.0 - RELAX) * c + (RELAX / 6.0) * (near - dv[row, t : t + 8, :])
            dst[row, t : t + 8, :] = val

    def inner(levels, k, first):
        @pl.loop(0, 2)
        def _(side):
            sweep_row(levels[k - 1], levels[k], 5 + side, first and k == 1)

    def wave(levels, j, first):
        for k in range(1, j + 1):
            d = j - k

            @pl.loop(0, 2)
            def _(side):
                sweep_row(levels[k - 1], levels[k], 4 - d + side * (3 + 2 * d), first and k == 1)

        if j < 4:
            inner(levels, j + 1, first)

    stage = (dv, a1, a2, a3, a4)
    moving = ship(dv, 0, (1, 2, 3, 4))
    inner(stage, 1, True)

    acc = jnp.zeros((1, 256), jnp.float32)
    for i in range(4):
        ramp = 1.0 + (sp * 4 + i).astype(jnp.float32) * (2.0 / 31.0)
        for h in range(2):
            lanes = slice(h * 256, (h + 1) * 256)
            gap = fore[3, i * 8 + 6 + h, 7:8, :] - obs[i : i + 1, lanes]
            acc = acc + gap * gap * (prec[i : i + 1, lanes] * ramp)
    parts[sp] = jnp.broadcast_to(jnp.sum(acc, axis=1, keepdims=True), (1, 128))
    for where in mates:
        small(parts.at[sp], parts.at[sp], 1, where).start()

    for j in (1, 2, 3):
        land(moving[j])
        wave(stage, j, True)
    later = ship(a4, 1, (2, 3))
    land(moving[4])
    wave(stage, 4, True)
    later.update(ship(a4, 1, (1, 4)))

    stage2 = (a4, a1, a2, a3, a8)
    inner(stage2, 1, False)

    small(picks.at[pl.ds(0, NPEER - 1)], picks.at[pl.ds(0, NPEER - 1)], 0, after).wait()
    start_second(0)

    for j in (2, 3, 1):
        land(later[j])
    for j in (1, 2, 3):
        wave(stage2, j, False)
    land(later[4])
    wave(stage2, 4, False)
    last = ship(a8, 2, (1,))

    @pl.loop(0, 4)
    def _(i):
        for zb in range(4):
            s = 8 * zb
            t = Z0 + s
            c = a8[i + 4, t : t + 8, :]
            put(1, i, zb, sv[i, s : s + 8, :] - 0.5 * (north(c, -1) - north(c, 1)))
            grad = a8[i + 4, t + 1 : t + 9, :] - a8[i + 4, t - 1 : t + 7, :]
            put(2, i, zb, sw[i, t : t + 8, :] - 0.5 * grad)

    start_first(1)

    land(last[1])

    @pl.loop(0, 4)
    def _(i):
        for zb in range(4):
            s = 8 * zb
            t = Z0 + s
            grad = a8[i + 5, t : t + 8, :] - a8[i + 3, t : t + 8, :]
            put(0, i, zb, su[i + 1, s : s + 8, :] - 0.5 * grad)

    start_first(2)

    small(parts.at[pl.ds(0, 7)], parts.at[pl.ds(0, 7)], 1, after).wait()
    mis = parts[0]
    for k in range(1, 8):
        mis = mis + parts[k]
    totals[me] = -0.5 * mis
    for _, where in peers:
        small(totals.at[me], totals.at[me], 2, where).start()

    start_second(1)

    small(totals.at[pl.ds(0, NPEER - 1)], totals.at[pl.ds(0, NPEER - 1)], 2, after).wait()
    a = totals[0:16]
    b = totals[16:32]
    top = jnp.maximum(a, b)
    isle = top + jnp.log(jnp.exp(a - top) + jnp.exp(b - top))
    peak = jnp.max(isle, axis=0)
    whole = peak + jnp.log(jnp.sum(jnp.exp(isle - peak[None]), axis=0))
    own = totals[isl]
    other = totals[isl + 16]
    top1 = jnp.maximum(own, other)
    mine = top1 + jnp.log(jnp.exp(own - top1) + jnp.exp(other - top1))
    logp[...] = totals[me] - mine
    logi[...] = mine - whole

    start_second(2)

    for f in range(4):
        for edge in edges[f]:
            edge.wait_send()
    for group in (moving, later, last):
        for copies in group.values():
            for copy in copies:
                copy.wait_send()
    for g in range(3):
        all_of(g, s1, r1).wait_send()
        all_of(g, s2, r2).wait()


def step(ensemble, observations, obs_precision, island_ancestor, particle_ancestor):
    field = ensemble[0, 0]
    vmem = pl.BlockSpec(memory_space=pltpu.VMEM)
    smem = pl.BlockSpec(memory_space=pltpu.SMEM)
    f32 = jnp.float32
    tall = Z0 + NZ + 8
    dma = pltpu.SemaphoreType.DMA
    out, logp, logi = pl.pallas_call(
        kernel,
        out_shape=(
            pltpu.VMEM(field.shape, f32),
            jax.ShapeDtypeStruct((1, 128), f32),
            jax.ShapeDtypeStruct((1, 128), f32),
        ),
        in_specs=[smem, smem, vmem, vmem, pl.BlockSpec(memory_space=pl.ANY)],
        out_specs=(vmem, vmem, vmem),
        scratch_shapes=[pltpu.VMEM((10, tall, LANES), f32) for _ in range(4)]
        + [
            pltpu.VMEM((6, NZ, LANES), f32),
            pltpu.VMEM((4, NZ, LANES), f32),
            pltpu.VMEM((4, tall, LANES), f32),
        ]
        + [pltpu.VMEM((12, tall, LANES), f32) for _ in range(6)]
        + [pltpu.VMEM((4, NPEER, 8, 256), f32)]
        + [pltpu.VMEM((NPEER, n, 8, 256), f32) for _, n in GROUPS + GROUPS]
        + [
            pltpu.VMEM((NPEER, 1, 128), f32),
            pltpu.VMEM((8, 1, 128), f32),
            pltpu.VMEM((NPEER, 1, 128), f32),
            dma((4,)),
            dma((4, 2)),
            dma((4, 2)),
            dma((3, 5, 2)),
            dma((3, 5, 2)),
            dma((3,)),
            dma((3,)),
            dma((3,)),
            dma((3,)),
            dma((3,)),
            dma((3,)),
            pltpu.SemaphoreType.REGULAR((3,)),
        ],
        compiler_params=pltpu.CompilerParams(
            collective_id=0, has_side_effects=True, vmem_limit_bytes=56 * 1024 * 1024
        ),
    )(island_ancestor, particle_ancestor, observations, obs_precision, field)
    return out[None, None], logp[:, :1], logi[0, :1]


def solution(mesh):
    return jax.shard_map(
        step,
        mesh=mesh,
        in_specs=(
            P("isl", "par", None, "sp", None, None),
            P("sp", None),
            P("sp", None),
            P(),
            P("isl", "par"),
        ),
        out_specs=(P("isl", "par", None, "sp", None, None), P("isl", "par"), P("isl")),
        check_vma=False,
    )
```

```python
import jax
import jax.numpy as jnp
from jax import lax
from jax.experimental import pallas as pl
from jax.experimental.pallas import tpu as pltpu
from jax.sharding import PartitionSpec as P

MESH = pl.DeviceIdType.MESH
NPEER = 32
GROUPS = ((3, 1), (1, 2), (0, 1))
STEP = 0.2
VISC = 0.05
STRAT = 1.0
RELAX = 0.8
Z0 = 8
FAR_FIRST = sorted(
    [(dz, dx) for dz in range(8) for dx in range(4) if dz or dx],
    key=lambda k: -(min(k[0], 8 - k[0]) + min(k[1], 4 - k[1])),
)
NZ = 32
LANES = 512


def north(q, k):
    return pltpu.roll(q, k % LANES, 1)


def pad_rows(ref, rows):
    zero = jnp.zeros((4, 8, 128), jnp.float32)

    @pl.loop(0, rows)
    def _(r):
        ref[r, :, 0:Z0, :] = zero
        ref[r, :, Z0 + NZ : Z0 + NZ + 8, :] = zero


def level(q, r, k, off=0):
    rows = pl.ds(Z0 + k + off, 8, stride=4)
    return jnp.concatenate([q[r, lane, rows, :] for lane in range(4)], axis=1)


def upper(tile):
    place = lax.broadcasted_iota(jnp.int32, tile.shape, 0)
    return jnp.where(place == 7, 0.0, pltpu.roll(tile, 7, 0))


def lower(tile):
    place = lax.broadcasted_iota(jnp.int32, tile.shape, 0)
    return jnp.where(place == 0, 0.0, pltpu.roll(tile, 1, 0))


def chunk_of(ref, first, count, flat):
    row = flat // 8
    lane = pl.multiple_of((flat // 2) % 4 * 128, 128)
    start = pl.multiple_of(flat % 2 * 16, 16)
    return ref.at[pl.ds(first, count), row, pl.ds(start, 16), pl.ds(lane, 128)]


def kernel(
    anc_far, pick, obs_far, prec_far, ens, out, logp, logi,
    xu, xv, xw, xb, su, sv, sw, dv, a1, a2, a3, a4, a8, fore,
    h0, h1, h2, g0, g1, g2, picks, parts, totals,
    anc, obs, prec, lsem, hs, hr, ws, wr, s1, r1, s2, r2, ssem, rsem, met,
):
    held = (h0, h1, h2)
    sent = (g0, g1, g2)
    isl = lax.axis_index("isl")
    par = lax.axis_index("par")
    sp = lax.axis_index("sp")
    me = par * 16 + isl
    z = par * 4 + lax.div(isl, 4)
    x = lax.rem(isl, 4)
    after = {"sp": lax.rem(sp + 1, 8)}
    before = {"sp": lax.rem(sp + 7, 8)}
    fields = (xu, xv, xw, xb)

    zs = []
    for dz in range(8):
        zt = lax.rem(z + dz, 8)
        zs.append((zt, lax.rem(zt, 4) * 4, lax.div(zt, 4)))
    xs = [lax.rem(x + dx, 4) for dx in range(4)]

    def away(dz, dx):
        zt, zlo4, hi = zs[dz % 8]
        return {"isl": zlo4 + xs[dx % 4], "par": hi}

    peers = []
    for dz, dx in FAR_FIRST:
        peers.append((zs[dz][0] * 4 + xs[dx], away(dz, dx)))
    mates = [{"sp": lax.rem(sp + k, 8)} for k in range(1, 8)]

    def tell(sem, where):
        pl.semaphore_signal(sem, inc=1, device_id=where, device_id_type=MESH)

    barrier = pltpu.get_barrier_semaphore()
    close = (after, before, away(0, 1), away(0, 3), away(1, 0), away(7, 0))
    for where in close:
        tell(barrier, where)

    loads = [
        pltpu.make_async_copy(
            ens.at[f, :, :, pl.ds(lane * 128, 128)], fields[f].at[3:7, lane, Z0 : Z0 + NZ, :], lsem.at[f, lane]
        )
        for f in (3, 1, 2, 0)
        for lane in range(4)
    ]
    loads += [
        pltpu.make_async_copy(obs_far, obs, lsem.at[4, 0]),
        pltpu.make_async_copy(prec_far, prec, lsem.at[4, 1]),
        pltpu.make_async_copy(anc_far, anc, lsem.at[4, 2]),
    ]
    for load in loads:
        load.start()

    def remote(src, dst, ss, rs, where):
        return pltpu.make_async_remote_copy(
            src_ref=src, dst_ref=dst, send_sem=ss, recv_sem=rs, device_id=where, device_id_type=MESH
        )

    def small(src, dst, sem, where):
        return remote(src, dst, ssem.at[sem], rsem.at[sem], where)

    pl.semaphore_wait(barrier, len(close))

    edges = {}
    for f in (3, 1, 2, 0):
        w = 3 if f == 0 else 2
        edges[f] = []
        for lane in range(4):
            cut = pl.ds(lane * 128, 128)
            into = fields[f].at[:, lane, Z0 : Z0 + NZ, :]
            edges[f] += [
                remote(
                    ens.at[f, 4 - w : 4, :, cut], into.at[3 - w : 3], hs.at[f, 0, lane], hr.at[f, 0, lane], after
                ),
                remote(ens.at[f, 0:w, :, cut], into.at[7 : 7 + w], hs.at[f, 1, lane], hr.at[f, 1, lane], before),
            ]
        for edge in edges[f]:
            edge.start()

    rounds = (
        (away(1, 0), away(7, 0), away(0, 1), away(0, 3), after, before),
        (away(2, 0), away(6, 0), mates[1], mates[5]),
        (away(0, 1), away(0, 3), away(0, 2)),
    )

    def call(k):
        for where in rounds[k]:
            tell(met.at[k], where)

    def hear(k):
        pl.semaphore_wait(met.at[k], len(rounds[k]))

    call(0)
    pad_rows(xb, 10)
    pad_rows(xv, 10)
    pad_rows(xw, 10)
    pad_rows(xu, 10)
    hear(0)
    call(1)
    picks[me] = jnp.full((1, 128), pick[0, 0], jnp.int32).astype(jnp.float32)
    hear(1)
    call(2)

    def land(copies):
        for copy in copies:
            copy.wait_recv()

    def tendency(q, r, k, u, v, w):
        c = level(q, r, k, 0)
        xp = level(q, r + 1, k, 0)
        xm = level(q, r - 1, k, 0)
        xpp = level(q, r + 2, k, 0)
        xmm = level(q, r - 2, k, 0)
        zp = level(q, r, k, 1)
        zm = level(q, r, k, -1)
        zpp = level(q, r, k, 2)
        zmm = level(q, r, k, -2)
        yp = north(c, -1)
        ym = north(c, 1)
        ypp = north(c, -2)
        ymm = north(c, 2)
        lap = (xp + xm) + (yp + ym) + (zp + zm) - 6.0 * c
        adv = (
            u * (8.0 * (xp - xm) - (xpp - xmm))
            + v * (8.0 * (yp - ym) - (ypp - ymm))
            + w * (8.0 * (zp - zm) - (zpp - zmm))
        )
        return c, (STEP * VISC) * lap - adv

    def put(f, i, k, value):
        for lane in range(4):
            fore[f, pl.ds((i * 4 + lane) * NZ + k, 8, stride=4), :] = value[:, lane * 128 : (lane + 1) * 128]

    def winds(r, k):
        return tuple(level(q, r, k, 0) * (STEP / 12.0) for q in (xu, xv, xw))

    def first_copy(g, flat, where):
        f, n = GROUPS[g]
        return remote(fore.at[pl.ds(f, n), pl.ds(pl.multiple_of(flat * 16, 16), 16), :], held[g].at[me], s1.at[g], r1.at[g], where)

    def second_copy(g, flat, where):
        f, n = GROUPS[g]
        return remote(sent[g].at[flat], chunk_of(out, f, n, me), s2.at[g], r2.at[g], where)

    def all_of(g, s, r):
        return remote(
            sent[g].at[pl.ds(0, NPEER - 1)], held[g].at[pl.ds(0, NPEER - 1)], s.at[g], r.at[g], after
        )

    def start_first(g):
        f, n = GROUPS[g]
        for flat, where in peers:
            first_copy(g, flat, where).start()
        held[g][me] = fore[pl.ds(f, n), pl.ds(pl.multiple_of(me * 16, 16), 16), :]

    def start_second(g):
        f, n = GROUPS[g]
        all_of(g, s1, r1).wait_recv()

        @pl.loop(0, NPEER)
        def _(d):
            src = anc[lax.rem(d, 16)]
            choose = jnp.broadcast_to(picks[d][None], (n, 16, 128)) < 0.5
            sent[g][d] = jnp.where(choose, held[g][src], held[g][src + 16])

        for flat, where in peers:
            second_copy(g, flat, where).start()
        chunk_of(out, f, n, me)[...] = sent[g][me]

    for load in loads:
        load.wait()
    land(edges[3])

    @pl.loop(0, 4)
    def _(i):
        r = i + 3
        for k in range(4):
            u, v, w = winds(r, k)
            c, g = tendency(xb, r, k, u, v, w)
            put(3, i, k, c + g - (STEP * STRAT) * level(xw, r, k, 0))

    hear(2)
    start_first(0)
    for _, where in peers:
        small(picks.at[me], picks.at[me], 0, where).start()

    land(edges[1])

    @pl.loop(0, 4)
    def _(i):
        r = i + 3
        for k in range(4):
            u, v, w = winds(r, k)
            c, g = tendency(xv, r, k, u, v, w)
            star = c + g
            sv[i, 8 * k : 8 * k + 8, :] = star
            dv[i + 4, 8 * k : 8 * k + 8, :] = 0.5 * (north(star, -1) - north(star, 1))

    land(edges[2])

    @pl.loop(0, 4)
    def _(i):
        r = i + 3
        for k in range(4):
            u, v, w = winds(r, k)
            c, g = tendency(xw, r, k, u, v, w)
            star = c + g + STEP * level(xb, r, k, 0)
            sw[i, 8 * k : 8 * k + 8, :] = star
        tiles = [sw[i, 8 * k : 8 * k + 8, :] for k in range(4)]
        above = (tiles[1], tiles[2], tiles[3], upper(tiles[0]))
        below = (lower(tiles[3]), tiles[0], tiles[1], tiles[2])
        for k in range(4):
            dv[i + 4, 8 * k : 8 * k + 8, :] = dv[i + 4, 8 * k : 8 * k + 8, :] + 0.5 * (above[k] - below[k])

    land(edges[0])

    @pl.loop(0, 6)
    def _(i):
        r = i + 2
        for k in range(4):
            u, v, w = winds(r, k)
            c, g = tendency(xu, r, k, u, v, w)
            su[i, 8 * k : 8 * k + 8, :] = c + g

    @pl.loop(0, 4)
    def _(i):
        for k in range(4):
            s = slice(8 * k, 8 * k + 8)
            dv[i + 4, s, :] = dv[i + 4, s, :] + 0.5 * (su[i + 2, s, :] - su[i, s, :])

    def ship(buf, e, away_rows):
        copies = {}
        for j in away_rows:
            copies[j] = (
                remote(
                    buf.at[8 - j], buf.at[4 - j], ws.at[e, j, 0], wr.at[e, j, 0], after
                ),
                remote(
                    buf.at[3 + j], buf.at[7 + j], ws.at[e, j, 1], wr.at[e, j, 1], before
                ),
            )
            for copy in copies[j]:
                copy.start()
        return copies

    def sweep_row(src, dst, row, first):
        tiles = [src[row, 8 * k : 8 * k + 8, :] for k in range(4)]
        above = (tiles[1], tiles[2], tiles[3], upper(tiles[0]))
        below = (lower(tiles[3]), tiles[0], tiles[1], tiles[2])
        for k in range(4):
            s = slice(8 * k, 8 * k + 8)
            c = tiles[k]
            near = (src[row + 1, s, :] + src[row - 1, s, :]) + (north(c, 1) + north(c, -1)) + (above[k] + below[k])
            if first:
                m = -RELAX / 6.0
                val = (m * (1.0 - RELAX) - RELAX / 6.0) * c + (m * RELAX / 6.0) * near
            else:
                val = (1.0 - RELAX) * c + (RELAX / 6.0) * (near - dv[row, s, :])
            dst[row, s, :] = val

    def inner(levels, k, first):
        for row in (5, 6):
            sweep_row(levels[k - 1], levels[k], row, first and k == 1)

    def wave(levels, j, first):
        for k in range(1, j + 1):
            for row in (4 - j + k, 7 + j - k):
                sweep_row(levels[k - 1], levels[k], row, first and k == 1)

        if j < 4:
            inner(levels, j + 1, first)

    stage = (dv, a1, a2, a3, a4)
    moving = ship(dv, 0, (1, 2, 3, 4))
    inner(stage, 1, True)

    acc = jnp.zeros((1, 128), jnp.float32)
    for i in range(4):
        ramp = 1.0 + (sp * 4 + i).astype(jnp.float32) * (2.0 / 31.0)
        for lane in range(4):
            lanes = slice(lane * 128, (lane + 1) * 128)
            top_row = (i * 4 + lane) * NZ + NZ - 1
            gap = fore[3, top_row : top_row + 1, :] - obs[i : i + 1, lanes]
            acc = acc + gap * gap * (prec[i : i + 1, lanes] * ramp)
    parts[sp] = jnp.broadcast_to(jnp.sum(acc, axis=1, keepdims=True), (1, 128))
    for where in mates:
        small(parts.at[sp], parts.at[sp], 1, where).start()

    for j in (1, 2, 3):
        land(moving[j])
        wave(stage, j, True)
    later = ship(a4, 1, (2, 3))
    land(moving[4])
    wave(stage, 4, True)
    later.update(ship(a4, 1, (1, 4)))

    stage2 = (a4, a1, a2, a3, a8)
    inner(stage2, 1, False)

    small(picks.at[pl.ds(0, NPEER - 1)], picks.at[pl.ds(0, NPEER - 1)], 0, after).wait()
    start_second(0)

    for j in (2, 3, 1):
        land(later[j])
    for j in (1, 2, 3):
        wave(stage2, j, False)
    land(later[4])
    wave(stage2, 4, False)
    last = ship(a8, 2, (1,))

    @pl.loop(0, 4)
    def _(i):
        tiles = [a8[i + 4, 8 * k : 8 * k + 8, :] for k in range(4)]
        above = (tiles[1], tiles[2], tiles[3], upper(tiles[0]))
        below = (lower(tiles[3]), tiles[0], tiles[1], tiles[2])
        for k in range(4):
            s = slice(8 * k, 8 * k + 8)
            c = tiles[k]
            put(1, i, k, sv[i, s, :] - 0.5 * (north(c, -1) - north(c, 1)))
            put(2, i, k, sw[i, s, :] - 0.5 * (above[k] - below[k]))

    start_first(1)

    land(last[1])

    @pl.loop(0, 4)
    def _(i):
        for k in range(4):
            s = slice(8 * k, 8 * k + 8)
            put(0, i, k, su[i + 1, s, :] - 0.5 * (a8[i + 5, s, :] - a8[i + 3, s, :]))

    start_first(2)

    small(parts.at[pl.ds(0, 7)], parts.at[pl.ds(0, 7)], 1, after).wait()
    mis = parts[0]
    for k in range(1, 8):
        mis = mis + parts[k]
    totals[me] = -0.5 * mis
    for _, where in peers:
        small(totals.at[me], totals.at[me], 2, where).start()

    start_second(1)

    small(totals.at[pl.ds(0, NPEER - 1)], totals.at[pl.ds(0, NPEER - 1)], 2, after).wait()
    a = totals[0:16]
    b = totals[16:32]
    top = jnp.maximum(a, b)
    isle = top + jnp.log(jnp.exp(a - top) + jnp.exp(b - top))
    peak = jnp.max(isle, axis=0)
    whole = peak + jnp.log(jnp.sum(jnp.exp(isle - peak[None]), axis=0))
    own = totals[isl]
    other = totals[isl + 16]
    top1 = jnp.maximum(own, other)
    mine = top1 + jnp.log(jnp.exp(own - top1) + jnp.exp(other - top1))
    logp[...] = totals[me] - mine
    logi[...] = mine - whole

    start_second(2)

    for f in range(4):
        for edge in edges[f]:
            edge.wait_send()
    for group in (moving, later, last):
        for copies in group.values():
            for copy in copies:
                copy.wait_send()
    for g in range(3):
        all_of(g, s1, r1).wait_send()
        all_of(g, s2, r2).wait()


def step(ensemble, observations, obs_precision, island_ancestor, particle_ancestor):
    field = ensemble[0, 0]
    vmem = pl.BlockSpec(memory_space=pltpu.VMEM)
    smem = pl.BlockSpec(memory_space=pltpu.SMEM)
    far = pl.BlockSpec(memory_space=pl.ANY)
    f32 = jnp.float32
    tall = Z0 + NZ + 8
    dma = pltpu.SemaphoreType.DMA
    out, logp, logi = pl.pallas_call(
        kernel,
        out_shape=(
            pltpu.VMEM(field.shape, f32),
            pltpu.VMEM((1, 128), f32),
            pltpu.VMEM((1, 128), f32),
        ),
        in_specs=[far, smem, far, far, far],
        out_specs=(vmem, vmem, vmem),
        scratch_shapes=[pltpu.VMEM((10, 4, tall, 128), f32) for _ in range(4)]
        + [
            pltpu.VMEM((6, NZ, LANES), f32),
            pltpu.VMEM((4, NZ, LANES), f32),
            pltpu.VMEM((4, NZ, LANES), f32),
        ]
        + [pltpu.VMEM((12, NZ, LANES), f32) for _ in range(6)]
        + [pltpu.VMEM((4, NPEER * 16, 128), f32)]
        + [pltpu.VMEM((NPEER, n, 16, 128), f32) for _, n in GROUPS + GROUPS]
        + [
            pltpu.VMEM((NPEER, 1, 128), f32),
            pltpu.VMEM((8, 1, 128), f32),
            pltpu.VMEM((NPEER, 1, 128), f32),
            pltpu.SMEM((16,), jnp.int32),
            pltpu.VMEM((4, LANES), f32),
            pltpu.VMEM((4, LANES), f32),
            dma((5, 4)),
            dma((4, 2, 4)),
            dma((4, 2, 4)),
            dma((3, 5, 2)),
            dma((3, 5, 2)),
            dma((3,)),
            dma((3,)),
            dma((3,)),
            dma((3,)),
            dma((3,)),
            dma((3,)),
            pltpu.SemaphoreType.REGULAR((3,)),
        ],
        compiler_params=pltpu.CompilerParams(
            collective_id=0, has_side_effects=True, vmem_limit_bytes=56 * 1024 * 1024
        ),
    )(island_ancestor, particle_ancestor, observations, obs_precision, field)
    return out[None, None], logp[:, :1], logi[0, :1]


def solution(mesh):
    return jax.shard_map(
        step,
        mesh=mesh,
        in_specs=(
            P("isl", "par", None, "sp", None, None),
            P("sp", None),
            P("sp", None),
            P(),
            P("isl", "par"),
        ),
        out_specs=(P("isl", "par", None, "sp", None, None), P("isl", "par"), P("isl")),
        check_vma=False,
    )
```

```python
import jax
import jax.numpy as jnp
from jax import lax
from jax.experimental import pallas as pl
from jax.experimental.pallas import tpu as pltpu
from jax.sharding import PartitionSpec as P

MESH = pl.DeviceIdType.MESH
NPEER = 32
GROUPS = ((3, 1, 0, 8), (3, 1, 8, 8), (1, 2, 0, 16), (0, 1, 0, 16))
STEP = 0.2
VISC = 0.05
STRAT = 1.0
RELAX = 0.8
Z0 = 8
FAR_FIRST = sorted(
    [(dz, dx) for dz in range(8) for dx in range(4) if dz or dx],
    key=lambda k: -(min(k[0], 8 - k[0]) + min(k[1], 4 - k[1])),
)
NZ = 32
LANES = 512


def north(q, k):
    return pltpu.roll(q, k % LANES, 1)


def pad_rows(ref, rows):
    zero = jnp.zeros((4, 8, 128), jnp.float32)

    @pl.loop(0, rows)
    def _(r):
        ref[r, :, 0:Z0, :] = zero
        ref[r, :, Z0 + NZ : Z0 + NZ + 8, :] = zero


def level(q, r, k, off=0):
    rows = pl.ds(Z0 + k + off, 8, stride=4)
    return jnp.concatenate([q[r, lane, rows, :] for lane in range(4)], axis=1)


def upper(tile):
    place = lax.broadcasted_iota(jnp.int32, tile.shape, 0)
    return jnp.where(place == 7, 0.0, pltpu.roll(tile, 7, 0))


def lower(tile):
    place = lax.broadcasted_iota(jnp.int32, tile.shape, 0)
    return jnp.where(place == 0, 0.0, pltpu.roll(tile, 1, 0))


def chunk_of(ref, group, flat):
    field, count, first, levels = group
    row = flat // 8
    lane = pl.multiple_of((flat // 2) % 4 * 128, 128)
    start = pl.multiple_of(flat % 2 * 16 + first, 8)
    return ref.at[pl.ds(field, count), row, pl.ds(start, levels), pl.ds(lane, 128)]


def piece_of(ref, group, flat):
    field, count, first, levels = group
    start = pl.multiple_of(flat * 16 + first, 8)
    return ref.at[pl.ds(field, count), pl.ds(start, levels), :]


def kernel(
    anc_far, pick, obs_far, prec_far, ens, out, logp, logi,
    xu, xv, xw, xb, su, sv, sw, dv, a1, a2, a3, a4, a8, fore,
    h0, h1, h2, h3, g0, g1, g2, g3, picks, parts, totals,
    anc, obs, prec, lsem, hs, hr, ws, wr, s1, r1, s2, r2, ssem, rsem, met,
):
    held = (h0, h1, h2, h3)
    sent = (g0, g1, g2, g3)
    isl = lax.axis_index("isl")
    par = lax.axis_index("par")
    sp = lax.axis_index("sp")
    me = par * 16 + isl
    z = par * 4 + lax.div(isl, 4)
    x = lax.rem(isl, 4)
    after = {"sp": lax.rem(sp + 1, 8)}
    before = {"sp": lax.rem(sp + 7, 8)}
    fields = (xu, xv, xw, xb)

    zs = []
    for dz in range(8):
        zt = lax.rem(z + dz, 8)
        zs.append((zt, lax.rem(zt, 4) * 4, lax.div(zt, 4)))
    xs = [lax.rem(x + dx, 4) for dx in range(4)]

    def away(dz, dx):
        zt, zlo4, hi = zs[dz % 8]
        return {"isl": zlo4 + xs[dx % 4], "par": hi}

    peers = []
    for dz, dx in FAR_FIRST:
        peers.append((zs[dz][0] * 4 + xs[dx], away(dz, dx)))
    mates = [{"sp": lax.rem(sp + k, 8)} for k in range(1, 8)]

    def tell(sem, where):
        pl.semaphore_signal(sem, inc=1, device_id=where, device_id_type=MESH)

    barrier = pltpu.get_barrier_semaphore()
    close = (after, before, away(0, 1), away(0, 3), away(1, 0), away(7, 0))
    for where in close:
        tell(barrier, where)

    loads = [
        pltpu.make_async_copy(
            ens.at[f, :, :, pl.ds(lane * 128, 128)], fields[f].at[3:7, lane, Z0 : Z0 + NZ, :], lsem.at[f, lane]
        )
        for f in (3, 1, 2, 0)
        for lane in range(4)
    ]
    loads += [
        pltpu.make_async_copy(obs_far, obs, lsem.at[4, 0]),
        pltpu.make_async_copy(prec_far, prec, lsem.at[4, 1]),
        pltpu.make_async_copy(anc_far, anc, lsem.at[4, 2]),
    ]
    for load in loads:
        load.start()

    def remote(src, dst, ss, rs, where):
        return pltpu.make_async_remote_copy(
            src_ref=src, dst_ref=dst, send_sem=ss, recv_sem=rs, device_id=where, device_id_type=MESH
        )

    def small(src, dst, sem, where):
        return remote(src, dst, ssem.at[sem], rsem.at[sem], where)

    pl.semaphore_wait(barrier, len(close))

    edges = {}
    for e, f, near, far_ in ((3, 3, 0, 2), (1, 1, 0, 2), (2, 2, 0, 2), (0, 0, 0, 2), (4, 0, 2, 3)):
        edges[e] = []
        for lane in range(4):
            cut = pl.ds(lane * 128, 128)
            into = fields[f].at[:, lane, Z0 : Z0 + NZ, :]
            edges[e] += [
                remote(
                    ens.at[f, 4 - far_ : 4 - near, :, cut],
                    into.at[3 - far_ : 3 - near],
                    hs.at[e, 0, lane],
                    hr.at[e, 0, lane],
                    after,
                ),
                remote(
                    ens.at[f, near:far_, :, cut], into.at[7 + near : 7 + far_], hs.at[e, 1, lane], hr.at[e, 1, lane], before
                ),
            ]
        for edge in edges[e]:
            edge.start()

    rounds = (
        (away(1, 0), away(7, 0), away(0, 1), away(0, 3), after, before),
        (away(2, 0), away(6, 0), mates[1], mates[5]),
        (away(0, 1), away(0, 3), away(0, 2)),
    )

    def call(k):
        for where in rounds[k]:
            tell(met.at[k], where)

    def hear(k):
        pl.semaphore_wait(met.at[k], len(rounds[k]))

    call(0)
    pad_rows(xb, 10)
    pad_rows(xv, 10)
    pad_rows(xw, 10)
    pad_rows(xu, 10)
    hear(0)
    call(1)
    picks[me] = jnp.full((1, 128), pick[0, 0], jnp.int32).astype(jnp.float32)
    hear(1)
    call(2)

    def land(copies):
        for copy in copies:
            copy.wait_recv()

    def tendency(q, r, k, u, v, w):
        c = level(q, r, k, 0)
        xp = level(q, r + 1, k, 0)
        xm = level(q, r - 1, k, 0)
        xpp = level(q, r + 2, k, 0)
        xmm = level(q, r - 2, k, 0)
        zp = level(q, r, k, 1)
        zm = level(q, r, k, -1)
        zpp = level(q, r, k, 2)
        zmm = level(q, r, k, -2)
        yp = north(c, -1)
        ym = north(c, 1)
        ypp = north(c, -2)
        ymm = north(c, 2)
        lap = (xp + xm) + (yp + ym) + (zp + zm) - 6.0 * c
        adv = (
            u * (8.0 * (xp - xm) - (xpp - xmm))
            + v * (8.0 * (yp - ym) - (ypp - ymm))
            + w * (8.0 * (zp - zm) - (zpp - zmm))
        )
        return c, (STEP * VISC) * lap - adv

    def put(f, i, k, value):
        for lane in range(4):
            fore[f, pl.ds((i * 4 + lane) * NZ + k, 8, stride=4), :] = value[:, lane * 128 : (lane + 1) * 128]

    def winds(r, k):
        return tuple(level(q, r, k, 0) * (STEP / 12.0) for q in (xu, xv, xw))

    def first_copy(g, flat, where):
        return remote(piece_of(fore, GROUPS[g], flat), held[g].at[me], s1.at[g], r1.at[g], where)

    def second_copy(g, flat, where):
        return remote(sent[g].at[flat], chunk_of(out, GROUPS[g], me), s2.at[g], r2.at[g], where)

    def all_of(g, s, r):
        return remote(
            sent[g].at[pl.ds(0, NPEER - 1)], held[g].at[pl.ds(0, NPEER - 1)], s.at[g], r.at[g], after
        )

    def start_first(g):
        for flat, where in peers:
            first_copy(g, flat, where).start()
        held[g][me] = piece_of(fore, GROUPS[g], me)[...]

    def start_second(g):
        all_of(g, s1, r1).wait_recv()

        @pl.loop(0, NPEER)
        def _(d):
            src = anc[lax.rem(d, 16)]
            choose = jnp.broadcast_to(picks[d][None], held[g].shape[1:]) < 0.5
            sent[g][d] = jnp.where(choose, held[g][src], held[g][src + 16])

        for flat, where in peers:
            second_copy(g, flat, where).start()
        chunk_of(out, GROUPS[g], me)[...] = sent[g][me]

    for load in loads:
        load.wait()
    land(edges[3])

    @pl.loop(0, 4)
    def _(i):
        r = i + 3
        for k in range(4):
            u, v, w = winds(r, k)
            c, g = tendency(xb, r, k, u, v, w)
            put(3, i, k, c + g - (STEP * STRAT) * level(xw, r, k, 0))

    hear(2)
    for _, where in peers:
        small(picks.at[me], picks.at[me], 0, where).start()
    start_first(0)
    start_first(1)

    land(edges[1])

    @pl.loop(0, 4)
    def _(i):
        r = i + 3
        for k in range(4):
            u, v, w = winds(r, k)
            c, g = tendency(xv, r, k, u, v, w)
            star = c + g
            sv[i, 8 * k : 8 * k + 8, :] = star
            dv[i + 4, 8 * k : 8 * k + 8, :] = 0.5 * (north(star, -1) - north(star, 1))

    land(edges[2])

    @pl.loop(0, 4)
    def _(i):
        r = i + 3
        for k in range(4):
            u, v, w = winds(r, k)
            c, g = tendency(xw, r, k, u, v, w)
            star = c + g + STEP * level(xb, r, k, 0)
            sw[i, 8 * k : 8 * k + 8, :] = star
        tiles = [sw[i, 8 * k : 8 * k + 8, :] for k in range(4)]
        above = (tiles[1], tiles[2], tiles[3], upper(tiles[0]))
        below = (lower(tiles[3]), tiles[0], tiles[1], tiles[2])
        for k in range(4):
            dv[i + 4, 8 * k : 8 * k + 8, :] = dv[i + 4, 8 * k : 8 * k + 8, :] + 0.5 * (above[k] - below[k])

    land(edges[0])

    def ship(buf, e, away_rows):
        copies = {}
        for j in away_rows:
            copies[j] = (
                remote(
                    buf.at[8 - j], buf.at[4 - j], ws.at[e, j, 0], wr.at[e, j, 0], after
                ),
                remote(
                    buf.at[3 + j], buf.at[7 + j], ws.at[e, j, 1], wr.at[e, j, 1], before
                ),
            )
            for copy in copies[j]:
                copy.start()
        return copies

    def star_u(i):
        r = i + 2
        for k in range(4):
            u, v, w = winds(r, k)
            c, g = tendency(xu, r, k, u, v, w)
            su[i, 8 * k : 8 * k + 8, :] = c + g

    def add_x(i):
        for k in range(4):
            s = slice(8 * k, 8 * k + 8)
            dv[i + 4, s, :] = dv[i + 4, s, :] + 0.5 * (su[i + 2, s, :] - su[i, s, :])

    @pl.loop(1, 5)
    def _(i):
        star_u(i)

    add_x(1)
    add_x(2)
    moving = ship(dv, 0, (2,))
    land(edges[4])

    @pl.loop(0, 2)
    def _(side):
        star_u(side * 5)

    add_x(0)
    add_x(3)

    def sweep_row(src, dst, row, first):
        tiles = [src[row, 8 * k : 8 * k + 8, :] for k in range(4)]
        above = (tiles[1], tiles[2], tiles[3], upper(tiles[0]))
        below = (lower(tiles[3]), tiles[0], tiles[1], tiles[2])
        for k in range(4):
            s = slice(8 * k, 8 * k + 8)
            c = tiles[k]
            near = (src[row + 1, s, :] + src[row - 1, s, :]) + (north(c, 1) + north(c, -1)) + (above[k] + below[k])
            if first:
                m = -RELAX / 6.0
                val = (m * (1.0 - RELAX) - RELAX / 6.0) * c + (m * RELAX / 6.0) * near
            else:
                val = (1.0 - RELAX) * c + (RELAX / 6.0) * (near - dv[row, s, :])
            dst[row, s, :] = val

    def inner(levels, k, first):
        for row in (5, 6):
            sweep_row(levels[k - 1], levels[k], row, first and k == 1)

    def wave(levels, j, first):
        for k in range(1, j + 1):
            for row in (4 - j + k, 7 + j - k):
                sweep_row(levels[k - 1], levels[k], row, first and k == 1)

        if j < 4:
            inner(levels, j + 1, first)

    stage = (dv, a1, a2, a3, a4)
    moving.update(ship(dv, 0, (1, 3, 4)))
    inner(stage, 1, True)

    acc = jnp.zeros((1, 128), jnp.float32)
    for i in range(4):
        ramp = 1.0 + (sp * 4 + i).astype(jnp.float32) * (2.0 / 31.0)
        for lane in range(4):
            lanes = slice(lane * 128, (lane + 1) * 128)
            top_row = (i * 4 + lane) * NZ + NZ - 1
            gap = fore[3, top_row : top_row + 1, :] - obs[i : i + 1, lanes]
            acc = acc + gap * gap * (prec[i : i + 1, lanes] * ramp)
    parts[sp] = jnp.broadcast_to(jnp.sum(acc, axis=1, keepdims=True), (1, 128))
    for where in mates:
        small(parts.at[sp], parts.at[sp], 1, where).start()

    for j in (1, 2, 3):
        land(moving[j])
        wave(stage, j, True)
    later = ship(a4, 1, (2, 3))
    small(picks.at[pl.ds(0, NPEER - 1)], picks.at[pl.ds(0, NPEER - 1)], 0, after).wait()
    start_second(0)
    land(moving[4])
    wave(stage, 4, True)
    later.update(ship(a4, 1, (1, 4)))

    stage2 = (a4, a1, a2, a3, a8)
    inner(stage2, 1, False)

    start_second(1)

    for j in (2, 3, 1):
        land(later[j])
    for j in (1, 2, 3):
        wave(stage2, j, False)
    land(later[4])
    wave(stage2, 4, False)
    last = ship(a8, 2, (1,))

    @pl.loop(0, 4)
    def _(i):
        tiles = [a8[i + 4, 8 * k : 8 * k + 8, :] for k in range(4)]
        above = (tiles[1], tiles[2], tiles[3], upper(tiles[0]))
        below = (lower(tiles[3]), tiles[0], tiles[1], tiles[2])
        for k in range(4):
            s = slice(8 * k, 8 * k + 8)
            c = tiles[k]
            put(1, i, k, sv[i, s, :] - 0.5 * (north(c, -1) - north(c, 1)))
            put(2, i, k, sw[i, s, :] - 0.5 * (above[k] - below[k]))

    start_first(2)

    land(last[1])

    @pl.loop(0, 4)
    def _(i):
        for k in range(4):
            s = slice(8 * k, 8 * k + 8)
            put(0, i, k, su[i + 1, s, :] - 0.5 * (a8[i + 5, s, :] - a8[i + 3, s, :]))

    start_first(3)

    small(parts.at[pl.ds(0, 7)], parts.at[pl.ds(0, 7)], 1, after).wait()
    mis = parts[0]
    for k in range(1, 8):
        mis = mis + parts[k]
    totals[me] = -0.5 * mis
    for _, where in peers:
        small(totals.at[me], totals.at[me], 2, where).start()

    start_second(2)

    small(totals.at[pl.ds(0, NPEER - 1)], totals.at[pl.ds(0, NPEER - 1)], 2, after).wait()
    a = totals[0:16]
    b = totals[16:32]
    top = jnp.maximum(a, b)
    isle = top + jnp.log(jnp.exp(a - top) + jnp.exp(b - top))
    peak = jnp.max(isle, axis=0)
    whole = peak + jnp.log(jnp.sum(jnp.exp(isle - peak[None]), axis=0))
    own = totals[isl]
    other = totals[isl + 16]
    top1 = jnp.maximum(own, other)
    mine = top1 + jnp.log(jnp.exp(own - top1) + jnp.exp(other - top1))
    logp[...] = totals[me] - mine
    logi[...] = mine - whole

    start_second(3)

    for f in range(5):
        for edge in edges[f]:
            edge.wait_send()
    for group in (moving, later, last):
        for copies in group.values():
            for copy in copies:
                copy.wait_send()
    for g in range(len(GROUPS)):
        all_of(g, s1, r1).wait_send()
        all_of(g, s2, r2).wait()


def step(ensemble, observations, obs_precision, island_ancestor, particle_ancestor):
    field = ensemble[0, 0]
    vmem = pl.BlockSpec(memory_space=pltpu.VMEM)
    smem = pl.BlockSpec(memory_space=pltpu.SMEM)
    far = pl.BlockSpec(memory_space=pl.ANY)
    f32 = jnp.float32
    tall = Z0 + NZ + 8
    dma = pltpu.SemaphoreType.DMA
    out, logp, logi = pl.pallas_call(
        kernel,
        out_shape=(
            pltpu.VMEM(field.shape, f32),
            pltpu.VMEM((1, 128), f32),
            pltpu.VMEM((1, 128), f32),
        ),
        in_specs=[far, smem, far, far, far],
        out_specs=(vmem, vmem, vmem),
        scratch_shapes=[pltpu.VMEM((10, 4, tall, 128), f32) for _ in range(4)]
        + [
            pltpu.VMEM((6, NZ, LANES), f32),
            pltpu.VMEM((4, NZ, LANES), f32),
            pltpu.VMEM((4, NZ, LANES), f32),
        ]
        + [pltpu.VMEM((12, NZ, LANES), f32) for _ in range(6)]
        + [pltpu.VMEM((4, NPEER * 16, 128), f32)]
        + [pltpu.VMEM((NPEER, n, levels, 128), f32) for _, n, _, levels in GROUPS + GROUPS]
        + [
            pltpu.VMEM((NPEER, 1, 128), f32),
            pltpu.VMEM((8, 1, 128), f32),
            pltpu.VMEM((NPEER, 1, 128), f32),
            pltpu.SMEM((16,), jnp.int32),
            pltpu.VMEM((4, LANES), f32),
            pltpu.VMEM((4, LANES), f32),
            dma((5, 4)),
            dma((5, 2, 4)),
            dma((5, 2, 4)),
            dma((3, 5, 2)),
            dma((3, 5, 2)),
            dma((4,)),
            dma((4,)),
            dma((4,)),
            dma((4,)),
            dma((3,)),
            dma((3,)),
            pltpu.SemaphoreType.REGULAR((3,)),
        ],
        compiler_params=pltpu.CompilerParams(
            collective_id=0, has_side_effects=True, vmem_limit_bytes=56 * 1024 * 1024
        ),
    )(island_ancestor, particle_ancestor, observations, obs_precision, field)
    return out[None, None], logp[:, :1], logi[0, :1]


def solution(mesh):
    return jax.shard_map(
        step,
        mesh=mesh,
        in_specs=(
            P("isl", "par", None, "sp", None, None),
            P("sp", None),
            P("sp", None),
            P(),
            P("isl", "par"),
        ),
        out_specs=(P("isl", "par", None, "sp", None, None), P("isl", "par"), P("isl")),
        check_vma=False,
    )
```

```python
import jax
import jax.numpy as jnp
from jax import lax
from jax.experimental import pallas as pl
from jax.experimental.pallas import tpu as pltpu
from jax.sharding import PartitionSpec as P

MESH = pl.DeviceIdType.MESH
NPEER = 32
GROUPS = ((3, 1, 0, 8), (3, 1, 8, 8), (1, 2, 0, 16), (0, 1, 0, 16))
STEP = 0.2
VISC = 0.05
STRAT = 1.0
RELAX = 0.8
Z0 = 8
FAR_FIRST = sorted(
    [(dz, dx) for dz in range(8) for dx in range(4) if dz or dx],
    key=lambda k: -(min(k[0], 8 - k[0]) + min(k[1], 4 - k[1])),
)
NZ = 32
LANES = 512


def north(q, k):
    return pltpu.roll(q, k % LANES, 1)


def pad_rows(ref, rows):
    zero = jnp.zeros((4, 8, 128), jnp.float32)

    @pl.loop(0, rows)
    def _(r):
        ref[r, :, 0:Z0, :] = zero
        ref[r, :, Z0 + NZ : Z0 + NZ + 8, :] = zero


def level(q, r, k, off=0):
    rows = pl.ds(Z0 + k + off, 8, stride=4)
    return jnp.concatenate([q[r, lane, rows, :] for lane in range(4)], axis=1)


def upper(tile):
    place = lax.broadcasted_iota(jnp.int32, tile.shape, 0)
    return jnp.where(place == 7, 0.0, pltpu.roll(tile, 7, 0))


def lower(tile):
    place = lax.broadcasted_iota(jnp.int32, tile.shape, 0)
    return jnp.where(place == 0, 0.0, pltpu.roll(tile, 1, 0))


def chunk_of(ref, group, flat):
    field, count, first, levels = group
    row = flat // 8
    lane = pl.multiple_of((flat // 2) % 4 * 128, 128)
    start = pl.multiple_of(flat % 2 * 16 + first, 8)
    return ref.at[pl.ds(field, count), row, pl.ds(start, levels), pl.ds(lane, 128)]


def piece_of(ref, group, flat):
    field, count, first, levels = group
    start = pl.multiple_of(flat * 16 + first, 8)
    return ref.at[pl.ds(field, count), pl.ds(start, levels), :]


def kernel(
    anc_far, pick, obs_far, prec_far, ens, out, logp, logi,
    xu, xv, xw, xb, su, sv, sw, dv, a1, a2, a3, a4, a8, fore,
    h0, h1, h2, h3, g0, g1, g2, g3, picks, parts, totals,
    anc, obs, prec, lsem, hs, hr, ws, wr, s1, r1, s2, r2, ssem, rsem, met,
):
    held = (h0, h1, h2, h3)
    sent = (g0, g1, g2, g3)
    isl = lax.axis_index("isl")
    par = lax.axis_index("par")
    sp = lax.axis_index("sp")
    me = par * 16 + isl
    z = par * 4 + lax.div(isl, 4)
    x = lax.rem(isl, 4)
    after = {"sp": lax.rem(sp + 1, 8)}
    before = {"sp": lax.rem(sp + 7, 8)}
    fields = (xu, xv, xw, xb)

    zs = []
    for dz in range(8):
        zt = lax.rem(z + dz, 8)
        zs.append((zt, lax.rem(zt, 4) * 4, lax.div(zt, 4)))
    xs = [lax.rem(x + dx, 4) for dx in range(4)]

    def away(dz, dx):
        zt, zlo4, hi = zs[dz % 8]
        return {"isl": zlo4 + xs[dx % 4], "par": hi}

    peers = []
    for dz, dx in FAR_FIRST:
        peers.append((zs[dz][0] * 4 + xs[dx], away(dz, dx)))
    mates = [{"sp": lax.rem(sp + k, 8)} for k in range(1, 8)]

    def tell(sem, where):
        pl.semaphore_signal(sem, inc=1, device_id=where, device_id_type=MESH)

    barrier = pltpu.get_barrier_semaphore()
    close = (after, before, away(0, 1), away(0, 3), away(1, 0), away(7, 0))
    for where in close:
        tell(barrier, where)

    loads = [
        pltpu.make_async_copy(
            ens.at[f, :, :, pl.ds(lane * 128, 128)], fields[f].at[3:7, lane, Z0 : Z0 + NZ, :], lsem.at[f, lane]
        )
        for f in (3, 1, 2, 0)
        for lane in range(4)
    ]
    loads += [
        pltpu.make_async_copy(obs_far, obs, lsem.at[4, 0]),
        pltpu.make_async_copy(prec_far, prec, lsem.at[4, 1]),
        pltpu.make_async_copy(anc_far, anc, lsem.at[4, 2]),
    ]
    for load in loads:
        load.start()

    def remote(src, dst, ss, rs, where):
        return pltpu.make_async_remote_copy(
            src_ref=src, dst_ref=dst, send_sem=ss, recv_sem=rs, device_id=where, device_id_type=MESH
        )

    def small(src, dst, sem, where):
        return remote(src, dst, ssem.at[sem], rsem.at[sem], where)

    pl.semaphore_wait(barrier, len(close))

    edges = {}
    for e, f, near, far_ in ((3, 3, 0, 2), (1, 1, 0, 2), (2, 2, 0, 2), (0, 0, 0, 2), (4, 0, 2, 3)):
        edges[e] = []
        for lane in range(4):
            cut = pl.ds(lane * 128, 128)
            into = fields[f].at[:, lane, Z0 : Z0 + NZ, :]
            edges[e] += [
                remote(
                    ens.at[f, 4 - far_ : 4 - near, :, cut],
                    into.at[3 - far_ : 3 - near],
                    hs.at[e, 0, lane],
                    hr.at[e, 0, lane],
                    after,
                ),
                remote(
                    ens.at[f, near:far_, :, cut], into.at[7 + near : 7 + far_], hs.at[e, 1, lane], hr.at[e, 1, lane], before
                ),
            ]
        for edge in edges[e]:
            edge.start()

    rounds = (
        (away(1, 0), away(7, 0), away(0, 1), away(0, 3), after, before),
        (away(2, 0), away(6, 0), mates[1], mates[5]),
        (away(0, 1), away(0, 3), away(0, 2)),
    )

    def call(k):
        for where in rounds[k]:
            tell(met.at[k], where)

    def hear(k):
        pl.semaphore_wait(met.at[k], len(rounds[k]))

    call(0)
    pad_rows(xb, 10)
    pad_rows(xv, 10)
    pad_rows(xw, 10)
    pad_rows(xu, 10)
    hear(0)
    call(1)
    picks[me] = jnp.full((1, 128), pick[0, 0], jnp.int32).astype(jnp.float32)
    hear(1)
    call(2)

    def land(copies):
        for copy in copies:
            copy.wait_recv()

    def tendency(q, r, k, u, v, w):
        c = level(q, r, k, 0)
        xp = level(q, r + 1, k, 0)
        xm = level(q, r - 1, k, 0)
        xpp = level(q, r + 2, k, 0)
        xmm = level(q, r - 2, k, 0)
        zp = level(q, r, k, 1)
        zm = level(q, r, k, -1)
        zpp = level(q, r, k, 2)
        zmm = level(q, r, k, -2)
        yp = north(c, -1)
        ym = north(c, 1)
        ypp = north(c, -2)
        ymm = north(c, 2)
        lap = (xp + xm) + (yp + ym) + (zp + zm) - 6.0 * c
        adv = (
            u * (8.0 * (xp - xm) - (xpp - xmm))
            + v * (8.0 * (yp - ym) - (ypp - ymm))
            + w * (8.0 * (zp - zm) - (zpp - zmm))
        )
        return c, (STEP * VISC) * lap - adv

    def put(f, i, k, value):
        for lane in range(4):
            fore[f, pl.ds((i * 4 + lane) * NZ + k, 8, stride=4), :] = value[:, lane * 128 : (lane + 1) * 128]

    def winds(r, k):
        return tuple(level(q, r, k, 0) * (STEP / 12.0) for q in (xu, xv, xw))

    def first_copy(g, flat, where):
        return remote(piece_of(fore, GROUPS[g], flat), held[g].at[me], s1.at[g], r1.at[g], where)

    def second_copy(g, flat, where):
        return remote(sent[g].at[flat], chunk_of(out, GROUPS[g], me), s2.at[g], r2.at[g], where)

    def all_of(g, s, r):
        return remote(
            sent[g].at[pl.ds(0, NPEER - 1)], held[g].at[pl.ds(0, NPEER - 1)], s.at[g], r.at[g], after
        )

    def start_first(g):
        for flat, where in peers:
            first_copy(g, flat, where).start()
        held[g][me] = piece_of(fore, GROUPS[g], me)[...]

    def start_second(g):
        all_of(g, s1, r1).wait_recv()

        @pl.loop(0, NPEER)
        def _(d):
            src = anc[lax.rem(d, 16)]
            choose = jnp.broadcast_to(picks[d][None], held[g].shape[1:]) < 0.5
            sent[g][d] = jnp.where(choose, held[g][src], held[g][src + 16])

        for flat, where in peers:
            second_copy(g, flat, where).start()
        chunk_of(out, GROUPS[g], me)[...] = sent[g][me]

    for load in loads:
        load.wait()
    land(edges[3])

    def star_b(i):
        r = i + 3
        for k in range(4):
            u, v, w = winds(r, k)
            c, g = tendency(xb, r, k, u, v, w)
            put(3, i, k, c + g - (STEP * STRAT) * level(xw, r, k, 0))

    @pl.loop(0, 2)
    def _(i):
        star_b(2 * i)
        star_b(2 * i + 1)

    hear(2)
    for _, where in peers:
        small(picks.at[me], picks.at[me], 0, where).start()
    start_first(0)
    start_first(1)

    land(edges[1])

    @pl.loop(0, 4)
    def _(i):
        r = i + 3
        for k in range(4):
            u, v, w = winds(r, k)
            c, g = tendency(xv, r, k, u, v, w)
            star = c + g
            sv[i, 8 * k : 8 * k + 8, :] = star
            dv[i + 4, 8 * k : 8 * k + 8, :] = 0.5 * (north(star, -1) - north(star, 1))

    land(edges[2])

    @pl.loop(0, 4)
    def _(i):
        r = i + 3
        for k in range(4):
            u, v, w = winds(r, k)
            c, g = tendency(xw, r, k, u, v, w)
            star = c + g + STEP * level(xb, r, k, 0)
            sw[i, 8 * k : 8 * k + 8, :] = star
        tiles = [sw[i, 8 * k : 8 * k + 8, :] for k in range(4)]
        above = (tiles[1], tiles[2], tiles[3], upper(tiles[0]))
        below = (lower(tiles[3]), tiles[0], tiles[1], tiles[2])
        for k in range(4):
            dv[i + 4, 8 * k : 8 * k + 8, :] = dv[i + 4, 8 * k : 8 * k + 8, :] + 0.5 * (above[k] - below[k])

    land(edges[0])

    def ship(buf, e, away_rows):
        copies = {}
        for j in away_rows:
            copies[j] = (
                remote(
                    buf.at[8 - j], buf.at[4 - j], ws.at[e, j, 0], wr.at[e, j, 0], after
                ),
                remote(
                    buf.at[3 + j], buf.at[7 + j], ws.at[e, j, 1], wr.at[e, j, 1], before
                ),
            )
            for copy in copies[j]:
                copy.start()
        return copies

    def star_u(i):
        r = i + 2
        for k in range(4):
            u, v, w = winds(r, k)
            c, g = tendency(xu, r, k, u, v, w)
            su[i, 8 * k : 8 * k + 8, :] = c + g

    def add_x(i):
        for k in range(4):
            s = slice(8 * k, 8 * k + 8)
            dv[i + 4, s, :] = dv[i + 4, s, :] + 0.5 * (su[i + 2, s, :] - su[i, s, :])

    @pl.loop(0, 2)
    def _(i):
        star_u(2 * i + 1)
        star_u(2 * i + 2)

    add_x(1)
    add_x(2)
    moving = ship(dv, 0, (2,))
    land(edges[4])

    star_u(0)
    star_u(5)

    add_x(0)
    add_x(3)

    def sweep_row(src, dst, row, first):
        tiles = [src[row, 8 * k : 8 * k + 8, :] for k in range(4)]
        above = (tiles[1], tiles[2], tiles[3], upper(tiles[0]))
        below = (lower(tiles[3]), tiles[0], tiles[1], tiles[2])
        for k in range(4):
            s = slice(8 * k, 8 * k + 8)
            c = tiles[k]
            near = (src[row + 1, s, :] + src[row - 1, s, :]) + (north(c, 1) + north(c, -1)) + (above[k] + below[k])
            if first:
                m = -RELAX / 6.0
                val = (m * (1.0 - RELAX) - RELAX / 6.0) * c + (m * RELAX / 6.0) * near
            else:
                val = (1.0 - RELAX) * c + (RELAX / 6.0) * (near - dv[row, s, :])
            dst[row, s, :] = val

    def inner(levels, k, first):
        for row in (5, 6):
            sweep_row(levels[k - 1], levels[k], row, first and k == 1)

    def wave(levels, j, first):
        for k in range(1, j + 1):
            for row in (4 - j + k, 7 + j - k):
                sweep_row(levels[k - 1], levels[k], row, first and k == 1)

        if j < 4:
            inner(levels, j + 1, first)

    stage = (dv, a1, a2, a3, a4)
    moving.update(ship(dv, 0, (1, 3, 4)))
    inner(stage, 1, True)

    acc = jnp.zeros((1, 128), jnp.float32)
    for i in range(4):
        ramp = 1.0 + (sp * 4 + i).astype(jnp.float32) * (2.0 / 31.0)
        for lane in range(4):
            lanes = slice(lane * 128, (lane + 1) * 128)
            top_row = (i * 4 + lane) * NZ + NZ - 1
            gap = fore[3, top_row : top_row + 1, :] - obs[i : i + 1, lanes]
            acc = acc + gap * gap * (prec[i : i + 1, lanes] * ramp)
    parts[sp] = jnp.broadcast_to(jnp.sum(acc, axis=1, keepdims=True), (1, 128))
    for where in mates:
        small(parts.at[sp], parts.at[sp], 1, where).start()

    for j in (1, 2, 3):
        land(moving[j])
        wave(stage, j, True)
    later = ship(a4, 1, (2, 3))
    small(picks.at[pl.ds(0, NPEER - 1)], picks.at[pl.ds(0, NPEER - 1)], 0, after).wait()
    start_second(0)
    land(moving[4])
    wave(stage, 4, True)
    later.update(ship(a4, 1, (1, 4)))

    stage2 = (a4, a1, a2, a3, a8)
    inner(stage2, 1, False)

    start_second(1)

    for j in (2, 3, 1):
        land(later[j])
    for j in (1, 2, 3):
        wave(stage2, j, False)
    land(later[4])
    wave(stage2, 4, False)
    last = ship(a8, 2, (1,))

    @pl.loop(0, 4)
    def _(i):
        tiles = [a8[i + 4, 8 * k : 8 * k + 8, :] for k in range(4)]
        above = (tiles[1], tiles[2], tiles[3], upper(tiles[0]))
        below = (lower(tiles[3]), tiles[0], tiles[1], tiles[2])
        for k in range(4):
            s = slice(8 * k, 8 * k + 8)
            c = tiles[k]
            put(1, i, k, sv[i, s, :] - 0.5 * (north(c, -1) - north(c, 1)))
            put(2, i, k, sw[i, s, :] - 0.5 * (above[k] - below[k]))

    start_first(2)

    land(last[1])

    @pl.loop(0, 4)
    def _(i):
        for k in range(4):
            s = slice(8 * k, 8 * k + 8)
            put(0, i, k, su[i + 1, s, :] - 0.5 * (a8[i + 5, s, :] - a8[i + 3, s, :]))

    start_first(3)

    small(parts.at[pl.ds(0, 7)], parts.at[pl.ds(0, 7)], 1, after).wait()
    mis = parts[0]
    for k in range(1, 8):
        mis = mis + parts[k]
    totals[me] = -0.5 * mis
    for _, where in peers:
        small(totals.at[me], totals.at[me], 2, where).start()

    start_second(2)

    small(totals.at[pl.ds(0, NPEER - 1)], totals.at[pl.ds(0, NPEER - 1)], 2, after).wait()
    a = totals[0:16]
    b = totals[16:32]
    top = jnp.maximum(a, b)
    isle = top + jnp.log(jnp.exp(a - top) + jnp.exp(b - top))
    peak = jnp.max(isle, axis=0)
    whole = peak + jnp.log(jnp.sum(jnp.exp(isle - peak[None]), axis=0))
    own = totals[isl]
    other = totals[isl + 16]
    top1 = jnp.maximum(own, other)
    mine = top1 + jnp.log(jnp.exp(own - top1) + jnp.exp(other - top1))
    logp[...] = totals[me] - mine
    logi[...] = mine - whole

    start_second(3)

    for f in range(5):
        for edge in edges[f]:
            edge.wait_send()
    for group in (moving, later, last):
        for copies in group.values():
            for copy in copies:
                copy.wait_send()
    for g in range(len(GROUPS)):
        all_of(g, s1, r1).wait_send()
        all_of(g, s2, r2).wait()


def step(ensemble, observations, obs_precision, island_ancestor, particle_ancestor):
    field = ensemble[0, 0]
    vmem = pl.BlockSpec(memory_space=pltpu.VMEM)
    smem = pl.BlockSpec(memory_space=pltpu.SMEM)
    far = pl.BlockSpec(memory_space=pl.ANY)
    f32 = jnp.float32
    tall = Z0 + NZ + 8
    dma = pltpu.SemaphoreType.DMA
    out, logp, logi = pl.pallas_call(
        kernel,
        out_shape=(
            pltpu.VMEM(field.shape, f32),
            pltpu.VMEM((1, 128), f32),
            pltpu.VMEM((1, 128), f32),
        ),
        in_specs=[far, smem, far, far, far],
        out_specs=(vmem, vmem, vmem),
        scratch_shapes=[pltpu.VMEM((10, 4, tall, 128), f32) for _ in range(4)]
        + [
            pltpu.VMEM((6, NZ, LANES), f32),
            pltpu.VMEM((4, NZ, LANES), f32),
            pltpu.VMEM((4, NZ, LANES), f32),
        ]
        + [pltpu.VMEM((12, NZ, LANES), f32) for _ in range(6)]
        + [pltpu.VMEM((4, NPEER * 16, 128), f32)]
        + [pltpu.VMEM((NPEER, n, levels, 128), f32) for _, n, _, levels in GROUPS + GROUPS]
        + [
            pltpu.VMEM((NPEER, 1, 128), f32),
            pltpu.VMEM((8, 1, 128), f32),
            pltpu.VMEM((NPEER, 1, 128), f32),
            pltpu.SMEM((16,), jnp.int32),
            pltpu.VMEM((4, LANES), f32),
            pltpu.VMEM((4, LANES), f32),
            dma((5, 4)),
            dma((5, 2, 4)),
            dma((5, 2, 4)),
            dma((3, 5, 2)),
            dma((3, 5, 2)),
            dma((4,)),
            dma((4,)),
            dma((4,)),
            dma((4,)),
            dma((3,)),
            dma((3,)),
            pltpu.SemaphoreType.REGULAR((3,)),
        ],
        compiler_params=pltpu.CompilerParams(
            collective_id=0, has_side_effects=True, vmem_limit_bytes=56 * 1024 * 1024
        ),
    )(island_ancestor, particle_ancestor, observations, obs_precision, field)
    return out[None, None], logp[:, :1], logi[0, :1]


def solution(mesh):
    return jax.shard_map(
        step,
        mesh=mesh,
        in_specs=(
            P("isl", "par", None, "sp", None, None),
            P("sp", None),
            P("sp", None),
            P(),
            P("isl", "par"),
        ),
        out_specs=(P("isl", "par", None, "sp", None, None), P("isl", "par"), P("isl")),
        check_vma=False,
    )
```
